32 devices in a mesh: gx: 8 (over z, x), gy: 4 (over y, core).
Axes of the slice: x: 2, y: 2, z: 4, core: 2. Of those that a mesh axis runs over, the one named last changes fastest.
Arguments:
- noise: bfloat16 [256, 512, 128], P('gy', 'gx'), may hold values from -6 to 6
- cheb_coeff: float32 [6], replicated, may hold values from 0.4 to 1.2
- diag_x: float32 [512, 64], P('gx'), may hold values from -0.165 to 0.165
- couple_x: bfloat16 [512, 64], P('gx'), may hold values from -0.1640625 to 0.1640625
- diag_y: float32 [256, 64], P('gy'), may hold values from -0.165 to 0.165
- couple_y: bfloat16 [256, 64], P('gy'), may hold values from -0.1640625 to 0.1640625
- track_rows: int32 [32], P('gy'), may hold values from 0 to 255, as said below
- track_obs: float32 [32, 512], P('gy', 'gx'), may hold values from -6 to 6
- weights: float32 [256, 32], P('gy'), may hold values from -1 to 1
Outputs:
- conditioned: float32 [256, 512, 128], P('gy', 'gx')
The draws below stay inside these ranges and needn't reach their ends.
Inputs may be any that keep to these rules, and one draw needn't show every extreme that they name: `track_rows`: in block j of 8 entries (j from 0) the entries are distinct rows of j * 64 to j * 64 + 63; the block's first entry is its first row where j is even and its last row where j is odd.
All inputs are finite; a program needn't handle non-finite values.
Results may differ from the reference program's by a relative error of at most 0.0055.
Values may be sent and summed in bfloat16 or wider, within the bound.
A program may use at most 64 MiB of HBM per device.

```python
import jax
import jax.numpy as jnp
from jax import lax

BLK = 64
SAMPLES = 128
TERMS = 6
TRK_DEV = 8
NX = 512
NY = 256
TRACKS = 32


def draw_track_rows(key, part):
    groups = TRACKS // TRK_DEV
    keys = jax.random.split(key, groups)

    def pick_rows(one_key):
        return jax.random.permutation(one_key, BLK - 2)[:TRK_DEV - 1]
    picks = jax.vmap(pick_rows)(keys).astype(jnp.int32) + 1
    index = jnp.arange(groups, dtype=jnp.int32)
    edge = index % 2 * (BLK - 1)
    rows = jnp.concatenate([edge[:, None], picks], axis=1) + index[:, None] * BLK
    return rows.reshape(-1).astype(jnp.int32)


def shard_levels(rng, dims, shards, low, largest):
    def one(axis_at, blocks):
        steps = jax.random.uniform(jax.random.fold_in(jax.random.fold_in(rng, 6), axis_at), (blocks,), jnp.float32, low / len(shards), largest / len(shards))
        return jnp.repeat(jnp.exp(steps), dims[axis_at] // blocks).reshape((-1,) + (1,) * (len(dims) - axis_at - 1))

    level = one(*shards[0])
    for cut in shards[1:]:
        level = level * one(*cut)
    return level


def normal_values(stream_key, extent, scale, reach, pieces=(), kind=jnp.bfloat16):
    entries = scale * jax.random.normal(stream_key, extent, jnp.float32)
    if pieces:
        entries = entries * shard_levels(stream_key, extent, pieces, -0.22, 0.18)
    return jnp.clip(entries, -reach, reach).astype(kind)


def setup_inputs(seed: int = 0) -> dict:
    seeds = jax.random.split(jax.random.key(seed), 10)
    noise = normal_values(seeds[0], (NY, NX, SAMPLES), 1.0, 6.0, ((0, 4), (1, 8)))
    cheb_coeff = jnp.clip(jax.random.uniform(seeds[1], (TERMS,), jnp.float32, 0.4, 1.2), 0.4, 1.2)
    diag_x = normal_values(seeds[2], (NX, BLK), (0.22 / BLK ** 0.5), 0.165, ((0, 8),), jnp.float32)
    couple_x = normal_values(seeds[3], (NX, BLK), (0.22 / BLK ** 0.5), 0.1640625, ((0, 8),))
    diag_y = normal_values(seeds[4], (NY, BLK), (0.22 / BLK ** 0.5), 0.165, ((0, 4),), jnp.float32)
    couple_y = normal_values(seeds[5], (NY, BLK), (0.22 / BLK ** 0.5), 0.1640625, ((0, 4),))
    track_rows = draw_track_rows(jax.random.fold_in(seeds[9], 71), 0)
    track_obs = normal_values(seeds[7], (TRACKS, NX), 1.0, 6.0, ((0, 4), (1, 8)), jnp.float32)
    weights = normal_values(seeds[8], (NY, TRACKS), TRACKS ** -0.5, 1.0, ((0, 4),), jnp.float32)
    return {"noise": noise, "cheb_coeff": cheb_coeff, "diag_x": diag_x, "couple_x": couple_x, "diag_y": diag_y, "couple_y": couple_y, "track_rows": track_rows, "track_obs": track_obs, "weights": weights}


NUGGET = 0.3


def round_keep(values):
    held = lax.optimization_barrier(values.astype(jnp.bfloat16))
    return held.astype(jnp.float32)


def apply_rows(field, diag_x, couple_x):
    xblocks = NX // BLK
    shaped = field.reshape(NY, xblocks, BLK, SAMPLES)
    inner = diag_x.reshape(xblocks, BLK, BLK)
    links = couple_x.reshape(xblocks, BLK, BLK).astype(jnp.float32)
    own = NUGGET * shaped + jnp.einsum("bij,ybjs->ybis", inner, shaped, precision=lax.Precision.HIGHEST)
    rounded = round_keep(shaped)
    empty = jnp.zeros((NY, 1, BLK, SAMPLES), jnp.float32)
    from_prev = jnp.einsum("bij,ybjs->ybis", links[1:], rounded[:, :-1], precision=lax.Precision.HIGHEST)
    from_next = jnp.einsum("bji,ybjs->ybis", links[1:], rounded[:, 1:], precision=lax.Precision.HIGHEST)
    from_prev = jnp.concatenate([empty, round_keep(from_prev)], axis=1)
    from_next = jnp.concatenate([round_keep(from_next), empty], axis=1)
    return (own + from_prev + from_next).reshape(NY, NX, SAMPLES)


def apply_cols(field, diag_y, couple_y):
    yblocks = NY // BLK
    shaped = field.reshape(yblocks, BLK, NX, SAMPLES)
    inner = diag_y.reshape(yblocks, BLK, BLK)
    links = couple_y.reshape(yblocks, BLK, BLK).astype(jnp.float32)
    own = NUGGET * shaped + jnp.einsum("bij,bjxs->bixs", inner, shaped, precision=lax.Precision.HIGHEST)
    rounded = round_keep(shaped)
    empty = jnp.zeros((1, BLK, NX, SAMPLES), jnp.float32)
    from_prev = jnp.einsum("bij,bjxs->bixs", links[1:], rounded[:-1], precision=lax.Precision.HIGHEST)
    from_next = jnp.einsum("bji,bjxs->bixs", links[1:], rounded[1:], precision=lax.Precision.HIGHEST)
    from_prev = jnp.concatenate([empty, round_keep(from_prev)], axis=0)
    from_next = jnp.concatenate([round_keep(from_next), empty], axis=0)
    return (own + from_prev + from_next).reshape(NY, NX, SAMPLES)


def reference(noise, cheb_coeff, diag_x, couple_x, diag_y, couple_y, track_rows, track_obs, weights):
    def operator(field):
        return apply_cols(apply_rows(field, diag_x, couple_x), diag_y, couple_y)

    start = noise.astype(jnp.float32)
    previous = start
    current = operator(start)
    total = cheb_coeff[0] * start
    total = total + cheb_coeff[1] * current
    for term in range(2, TERMS):
        following = 2.0 * operator(current) - previous
        previous = current
        current = following
        total = total + cheb_coeff[term] * current
    picked = jnp.take(total, track_rows.astype(jnp.int32), axis=0)
    misfit = picked - track_obs[:, :, None]
    correction = jnp.dot(weights, misfit.reshape(TRACKS, NX * SAMPLES), precision=lax.Precision.HIGHEST)
    return total - correction.reshape(NY, NX, SAMPLES)
```

```python
import jax
import jax.numpy as jnp
from jax import lax
from jax.experimental import pallas as pl
from jax.experimental.pallas import tpu as pltpu
from jax.sharding import PartitionSpec as P

NUGGET = 0.3


def padded_2(value, sides, width):
    for axis, dim in sides:
        size, length = (lax.axis_size(axis), value.shape[dim])
        up = [(i, (i + 1) % size) for i in range(size - 1)]
        down = [(j, i) for i, j in up]
        last = lax.slice_in_dim(value, length - width, length, axis=dim)
        leading = lax.slice_in_dim(value, 0, width, axis=dim)
        before = lax.ppermute(last, axis, up)
        after = lax.ppermute(leading, axis, down)
        value = jnp.concatenate([before, value, after], axis=dim)
    return value


def shifted(value, axis, steps):
    count = lax.axis_size(axis)
    leading, last = (max(0, -steps), min(count, count - steps))
    return lax.ppermute(value, axis, [(source, source + steps) for source in range(leading, last)])


def along_rows(matrix, field):
    return jnp.einsum("ij,yjs->yis", matrix, field, preferred_element_type=jnp.float32)


def along_rows_back(matrix, field):
    return jnp.einsum("ji,yjs->yis", matrix, field, preferred_element_type=jnp.float32)


def along_cols(matrix, field):
    flat = field.reshape(field.shape[0], -1)
    return jnp.dot(matrix, flat, preferred_element_type=jnp.float32).reshape(field.shape)


def along_cols_back(matrix, field):
    flat = field.reshape(field.shape[0], -1)
    return jnp.dot(matrix.T, flat, preferred_element_type=jnp.float32).reshape(field.shape)


def apply_rows(field, diag_x, couple_x, next_x):
    width = field.shape[1]
    own = NUGGET * field + jnp.einsum(
        "ij,yjs->yis",
        diag_x,
        field,
        precision=lax.Precision.HIGHEST,
        preferred_element_type=jnp.float32,
    )
    rounded = field.astype(jnp.bfloat16)
    padded = padded_2(rounded, (("gx", 1),), width)
    from_prev = along_rows(couple_x, padded[:, :width]).astype(jnp.bfloat16)
    from_next = along_rows_back(next_x, padded[:, 2 * width :]).astype(jnp.bfloat16)
    from_prev = lax.optimization_barrier(from_prev)
    from_next = lax.optimization_barrier(from_next)
    return own + from_prev.astype(jnp.float32) + from_next.astype(jnp.float32)


def apply_cols(field, diag_y, couple_y, next_y):
    height = field.shape[0]
    own = NUGGET * field + jnp.dot(
        diag_y,
        field.reshape(height, -1),
        precision=lax.Precision.HIGHEST,
        preferred_element_type=jnp.float32,
    ).reshape(field.shape)
    rounded = field.astype(jnp.bfloat16)
    padded = padded_2(rounded, (("gy", 0),), height)
    from_prev = along_cols(couple_y, padded[:height]).astype(jnp.bfloat16)
    from_next = along_cols_back(next_y, padded[2 * height :]).astype(jnp.bfloat16)
    from_prev = lax.optimization_barrier(from_prev)
    from_next = lax.optimization_barrier(from_next)
    return own + from_prev.astype(jnp.float32) + from_next.astype(jnp.float32)


def halo_body(noise, cheb_coeff, diag_x, couple_x, diag_y, couple_y, track_rows, track_obs, weights):
    next_x = shifted(couple_x, "gx", -1)
    next_y = shifted(couple_y, "gy", -1)

    def operator(field):
        return apply_cols(apply_rows(field, diag_x, couple_x, next_x), diag_y, couple_y, next_y)

    start = noise.astype(jnp.float32)
    terms = cheb_coeff.shape[0]
    previous = start
    current = operator(start)
    total = cheb_coeff[0] * start
    total = total + cheb_coeff[1] * current
    for term in range(2, terms):
        following = 2.0 * operator(current) - previous
        previous = current
        current = following
        total = total + cheb_coeff[term] * current
    height = total.shape[0]
    first_row = lax.axis_index("gy") * height
    local_rows = track_rows - first_row
    picked = jnp.take(total, local_rows, axis=0)
    misfit = picked - track_obs[:, :, None]
    piece = lax.all_gather(misfit.astype(jnp.bfloat16), "gy", axis=0, tiled=True).astype(
        jnp.float32
    )
    flat = piece.reshape(piece.shape[0], -1)
    correction = jnp.dot(
        weights, flat, precision=lax.Precision.HIGHEST, preferred_element_type=jnp.float32
    )
    return total - correction.reshape(total.shape)

LANES = 128
BF16 = jnp.bfloat16
F32 = jnp.float32


def halves(value):
    high = value.astype(BF16)
    return high, (value - high.astype(F32)).astype(BF16)


def offsets(count):
    return sorted(range(count), key=lambda k: -min(k, count - k))


def place(me, nx, ny, dx, dy):
    return (lax.rem(me[0] + dx, nx), lax.rem(me[1] + dy, ny))


def greet(nx, ny, me):
    barrier = pltpu.get_barrier_semaphore()
    for dx in range(nx):
        for dy in range(ny):
            if dx or dy:
                pl.semaphore_signal(barrier, inc=1, device_id=place(me, nx, ny, dx, dy))
    pl.semaphore_wait(barrier, nx * ny - 1)


def scatter_kernel(nx, ny, x_ref, gx_ref, gy_ref, v_ref, gxs_ref, gys_ref, local, send, recv, xsend, xrecv, ysend, yrecv):
    me = (lax.axis_index("gx"), lax.axis_index("gy"))
    pairs, height, _ = v_ref.shape
    height = height // ny
    own = (
        pltpu.make_async_copy(
            x_ref.at[pl.ds((me[0] * ny + me[1]) * pairs, pairs)],
            v_ref.at[:, pl.ds(me[1] * height, height), pl.ds(me[0] * LANES, LANES)],
            local.at[0],
        ),
        pltpu.make_async_copy(gx_ref, gxs_ref.at[me[0]], local.at[1]),
        pltpu.make_async_copy(gy_ref, gys_ref.at[me[1]], local.at[2]),
    )
    for copy in own:
        copy.start()
    greet(nx, ny, me)

    def block(dx, dy, at):
        to = place(me, nx, ny, dx, dy)
        return pltpu.make_async_remote_copy(
            src_ref=x_ref.at[pl.ds((to[0] * ny + to[1]) * pairs, pairs)],
            dst_ref=v_ref.at[:, pl.ds(at[1] * height, height), pl.ds(at[0] * LANES, LANES)],
            send_sem=send.at[dx * ny + dy],
            recv_sem=recv.at[dx * ny + dy],
            device_id=to,
        )

    def part_x(dx, at):
        return pltpu.make_async_remote_copy(
            src_ref=gx_ref, dst_ref=gxs_ref.at[at[0]], send_sem=xsend.at[dx], recv_sem=xrecv.at[dx],
            device_id=place(me, nx, ny, dx, 0),
        )

    def part_y(dy, at):
        return pltpu.make_async_remote_copy(
            src_ref=gy_ref, dst_ref=gys_ref.at[at[1]], send_sem=ysend.at[dy], recv_sem=yrecv.at[dy],
            device_id=place(me, nx, ny, 0, dy),
        )

    order = [(dx, dy) for dx in offsets(nx) for dy in offsets(ny) if dx or dy]
    for dx in offsets(nx):
        if dx:
            part_x(dx, me).start()
    for dx, dy in order:
        block(dx, dy, me).start()
    for dy in offsets(ny):
        if dy:
            part_y(dy, me).start()
    for dx in offsets(nx):
        if dx:
            part_x(dx, place(me, nx, ny, nx - dx, 0)).wait()
    for dy in offsets(ny):
        if dy:
            part_y(dy, place(me, nx, ny, 0, ny - dy)).wait()
    for dx, dy in order:
        block(dx, dy, place(me, nx, ny, nx - dx, ny - dy)).wait()
    for copy in own:
        copy.wait()


def gather_kernel(nx, ny, v_ref, y_ref, local, send, recv):
    me = (lax.axis_index("gx"), lax.axis_index("gy"))
    pairs, height, _ = v_ref.shape
    height = height // ny

    def source(at):
        return v_ref.at[:, pl.ds(at[1] * height, height), pl.ds(at[0] * LANES, LANES)]

    def target(at):
        return y_ref.at[pl.ds((at[0] * ny + at[1]) * pairs, pairs)]

    own = pltpu.make_async_copy(source(me), target(me), local.at[0])
    own.start()
    greet(nx, ny, me)

    def block(dx, dy, at):
        to = place(me, nx, ny, dx, dy)
        return pltpu.make_async_remote_copy(
            src_ref=source(to), dst_ref=target(at), send_sem=send.at[dx * ny + dy],
            recv_sem=recv.at[dx * ny + dy], device_id=to,
        )

    order = [(dx, dy) for dx in offsets(nx) for dy in offsets(ny) if dx or dy]
    for dx, dy in order:
        block(dx, dy, me).start()
    for dx, dy in order:
        block(dx, dy, place(me, nx, ny, nx - dx, ny - dy)).wait()
    own.wait()


def dot(a, b):
    return jnp.dot(a, b, preferred_element_type=F32)


def build_weights(nx, ny, width, tracks, gxs_ref, gys_ref, wx_ref, wy_ref, wp_ref):
    zero = jnp.zeros((width, width), F32)
    wx_ref[...] = jnp.zeros_like(wx_ref)
    wy_ref[...] = jnp.zeros_like(wy_ref)

    def put_x(out, inn, value):
        row = (inn - (out // 2 * 2 - 1)) * LANES
        lane = (out % 2) * LANES
        for half in range(2):
            sides = [value, zero] if half == 0 else [zero, value]
            wx_ref[out // 2, row + half * width : row + (half + 1) * width, lane : lane + LANES] = (
                jnp.concatenate(sides, axis=1).astype(BF16)
            )

    for b in range(nx):
        both = gxs_ref[b].astype(F32)
        turned = both.T
        put_x(b, b, turned[:width])
        if b:
            put_x(b, b - 1, turned[width:])
            put_x(b - 1, b, both[:, width:])
    blocks = [gys_ref[c, :width].astype(F32) for c in range(ny)]
    for c in range(ny):
        row = [zero] * ny
        row[c] = blocks[c][:, :width]
        if c:
            row[c - 1] = blocks[c][:, width:]
        if c < ny - 1:
            row[c + 1] = blocks[c + 1].T[width:]
        wy_ref[c * width : (c + 1) * width] = jnp.concatenate(row, axis=1).astype(BF16)
    extra = jnp.concatenate([gys_ref[c, width : 2 * width] for c in range(ny)], axis=0)
    hot = extra[:, 2 * tracks : 3 * tracks]
    for part in range(2):
        wp_ref[part] = lax.dot_general(
            extra[:, part * tracks : (part + 1) * tracks], hot, (((1,), (1,)), ((), ())),
            preferred_element_type=F32,
        ).astype(BF16)


def chebyshev(terms, wide, coeff_ref, wx_ref, wy_ref, wp_ref, cur, prev, total, u, cbf, ubf, emit):
    slab = 2 * LANES
    count = wide // slab
    cols = [slice(j * slab, (j + 1) * slab) for j in range(count)]

    def step(k, _):
        twice = jnp.where(k == 1, 1.0, 2.0)
        keep = jnp.where(k == 1, 0.0, 1.0)
        coeff = coeff_ref[k]
        for j in range(count):
            out = NUGGET * cur[:, cols[j]] + dot(cbf[:, j * slab : (j + 2) * slab], wx_ref[j])
            u[:, cols[j]] = out
            ubf[:, cols[j]] = out.astype(BF16)
        for j in range(count):
            out = NUGGET * u[:, cols[j]] + dot(wy_ref[...], ubf[:, cols[j]])
            old = cur[:, cols[j]]
            new = twice * out - keep * prev[:, cols[j]]
            prev[:, cols[j]] = old
            cur[:, cols[j]] = new
            total[:, cols[j]] += coeff * new
            cbf[:, LANES + j * slab : LANES + (j + 1) * slab] = new.astype(BF16)
        return 0

    lax.fori_loop(1, terms, step, 0)
    for j in range(count):
        field = total[:, cols[j]]
        high, low = halves(field)
        fix = dot(wp_ref[0], high) + dot(wp_ref[0], low) + dot(wp_ref[1], high)
        emit(cols[j], field - fix)


def sample_kernel(nx, ny, width, tracks, coeff_ref, v_ref, gxs_ref, gys_ref, out_ref, wx_ref, wy_ref, wp_ref, cur, prev, total, u, cbf, ubf):
    pairs, tall, wide = v_ref.shape
    build_weights(nx, ny, width, tracks, gxs_ref, gys_ref, wx_ref, wy_ref, wp_ref)
    cbf[:, :LANES] = jnp.zeros((tall, LANES), BF16)
    cbf[:, LANES + wide :] = jnp.zeros((tall, LANES), BF16)
    for pair in range(pairs):
        value = v_ref[pair]
        cbf[:, LANES : LANES + wide] = value
        start = value.astype(F32)
        cur[...] = start
        prev[...] = start
        total[...] = coeff_ref[0] * start

        def emit(col, value, pair=pair):
            out_ref[pair, :, col] = value.astype(BF16)

        chebyshev(coeff_ref.shape[0], wide, coeff_ref, wx_ref, wy_ref, wp_ref, cur, prev, total, u, cbf, ubf, emit)


def swap_body(nx, ny, noise, cheb_coeff, diag_x, couple_x, diag_y, couple_y, track_rows, track_obs, weights):
    height, width, samples = noise.shape
    tracks = weights.shape[1]
    per = track_rows.shape[0]
    lines = samples // 2
    pairs = lines // (nx * ny)
    tall, wide = ny * height, nx * LANES
    at = lax.axis_index("gy")
    x = noise.reshape(height, width, 2, lines).transpose(3, 0, 2, 1).reshape(lines, height, LANES)
    part_x = jnp.concatenate([diag_x.astype(BF16), couple_x], axis=1)
    member = jnp.arange(tracks) // per == at
    local = jnp.where(member, jnp.tile(track_rows, ny) - at * height, -1)
    hot = (jnp.arange(height)[:, None] == local[None, :]).astype(BF16)
    w_high, w_low = halves(weights)
    extra = jnp.concatenate([w_high, w_low, hot], axis=1)
    extra = jnp.pad(extra, ((0, 0), (0, LANES - extra.shape[1])))
    obs = jnp.concatenate(halves(track_obs), axis=1)
    obs = jnp.pad(obs, ((0, -per % 16), (0, 0)))
    part_y = jnp.concatenate([jnp.concatenate([diag_y.astype(BF16), couple_y], axis=1), extra, obs], axis=0)
    rows = part_y.shape[0]
    vmem = pl.BlockSpec(memory_space=pltpu.VMEM)
    dma = pltpu.SemaphoreType.DMA
    devices = nx * ny
    v, gxs, gys = pl.pallas_call(
        lambda *refs: scatter_kernel(nx, ny, *refs),
        out_shape=(
            jax.ShapeDtypeStruct((pairs, tall, wide), BF16),
            jax.ShapeDtypeStruct((nx, width, LANES), BF16),
            jax.ShapeDtypeStruct((ny, rows, LANES), BF16),
        ),
        in_specs=[vmem] * 3,
        out_specs=(vmem,) * 3,
        scratch_shapes=[dma((3,)), dma((devices,)), dma((devices,)), dma((nx,)), dma((nx,)), dma((ny,)), dma((ny,))],
        compiler_params=pltpu.CompilerParams(collective_id=0, has_side_effects=True),
        name="scatter",
    )(x, part_x, part_y)
    field = pltpu.VMEM((tall, wide), F32)
    out = pl.pallas_call(
        lambda *refs: sample_kernel(nx, ny, width, tracks, *refs),
        out_shape=jax.ShapeDtypeStruct((pairs, tall, wide), BF16),
        in_specs=[pl.BlockSpec(memory_space=pltpu.SMEM), vmem, vmem, vmem],
        out_specs=vmem,
        scratch_shapes=[
            pltpu.VMEM((nx // 2, 4 * LANES, 2 * LANES), BF16),
            pltpu.VMEM((tall, tall), BF16),
            pltpu.VMEM((2, tall, tall), BF16),
            field, field, field, field,
            pltpu.VMEM((tall, wide + 2 * LANES), BF16),
            pltpu.VMEM((tall, wide), BF16),
        ],
        name="sample",
    )(cheb_coeff, v, gxs, gys)
    y = pl.pallas_call(
        lambda *refs: gather_kernel(nx, ny, *refs),
        out_shape=jax.ShapeDtypeStruct((lines, height, LANES), BF16),
        in_specs=[vmem],
        out_specs=vmem,
        scratch_shapes=[dma((1,)), dma((devices,)), dma((devices,))],
        compiler_params=pltpu.CompilerParams(collective_id=1, has_side_effects=True),
        name="gather",
    )(out)
    seen = gys[:, 2 * height : 2 * height + per].astype(F32)
    seen = (seen[:, :, :width] + seen[:, :, width:]).reshape(tracks, width)
    level = jnp.dot(weights, seen, precision=lax.Precision.HIGHEST, preferred_element_type=F32)
    y = y.reshape(lines, height, 2, width).transpose(1, 3, 2, 0).reshape(height, width, samples)
    return y.astype(F32) + level[:, :, None]


def body(noise, *rest):
    nx, ny = lax.axis_size("gx"), lax.axis_size("gy")
    height, width, samples = noise.shape
    tracks, per = rest[-1].shape[1], rest[-3].shape[0]
    fits = 2 * width == LANES and height == width and nx % 2 == 0 and samples % (2 * nx * ny) == 0
    fits = fits and 3 * tracks <= LANES and per * ny == tracks
    if fits:
        return swap_body(nx, ny, noise, *rest)
    return halo_body(noise, *rest)


def solution(mesh):
    return jax.shard_map(
        body,
        mesh=mesh,
        in_specs=(
            P("gy", "gx", None),
            P(),
            P("gx", None),
            P("gx", None),
            P("gy", None),
            P("gy", None),
            P("gy"),
            P("gy", "gx"),
            P("gy", None),
        ),
        out_specs=P("gy", "gx", None),
        check_vma=False,
    )
```

```python
import jax
import jax.numpy as jnp
from jax import lax
from jax.experimental import pallas as pl
from jax.experimental.pallas import tpu as pltpu
from jax.sharding import PartitionSpec as P

NUGGET = 0.3


def padded_2(value, sides, width):
    for axis, dim in sides:
        size, length = (lax.axis_size(axis), value.shape[dim])
        up = [(i, (i + 1) % size) for i in range(size - 1)]
        down = [(j, i) for i, j in up]
        last = lax.slice_in_dim(value, length - width, length, axis=dim)
        leading = lax.slice_in_dim(value, 0, width, axis=dim)
        before = lax.ppermute(last, axis, up)
        after = lax.ppermute(leading, axis, down)
        value = jnp.concatenate([before, value, after], axis=dim)
    return value


def shifted(value, axis, steps):
    count = lax.axis_size(axis)
    leading, last = (max(0, -steps), min(count, count - steps))
    return lax.ppermute(value, axis, [(source, source + steps) for source in range(leading, last)])


def along_rows(matrix, field):
    return jnp.einsum("ij,yjs->yis", matrix, field, preferred_element_type=jnp.float32)


def along_rows_back(matrix, field):
    return jnp.einsum("ji,yjs->yis", matrix, field, preferred_element_type=jnp.float32)


def along_cols(matrix, field):
    flat = field.reshape(field.shape[0], -1)
    return jnp.dot(matrix, flat, preferred_element_type=jnp.float32).reshape(field.shape)


def along_cols_back(matrix, field):
    flat = field.reshape(field.shape[0], -1)
    return jnp.dot(matrix.T, flat, preferred_element_type=jnp.float32).reshape(field.shape)


def apply_rows(field, diag_x, couple_x, next_x):
    width = field.shape[1]
    own = NUGGET * field + jnp.einsum(
        "ij,yjs->yis",
        diag_x,
        field,
        precision=lax.Precision.HIGHEST,
        preferred_element_type=jnp.float32,
    )
    rounded = field.astype(jnp.bfloat16)
    padded = padded_2(rounded, (("gx", 1),), width)
    from_prev = along_rows(couple_x, padded[:, :width]).astype(jnp.bfloat16)
    from_next = along_rows_back(next_x, padded[:, 2 * width :]).astype(jnp.bfloat16)
    from_prev = lax.optimization_barrier(from_prev)
    from_next = lax.optimization_barrier(from_next)
    return own + from_prev.astype(jnp.float32) + from_next.astype(jnp.float32)


def apply_cols(field, diag_y, couple_y, next_y):
    height = field.shape[0]
    own = NUGGET * field + jnp.dot(
        diag_y,
        field.reshape(height, -1),
        precision=lax.Precision.HIGHEST,
        preferred_element_type=jnp.float32,
    ).reshape(field.shape)
    rounded = field.astype(jnp.bfloat16)
    padded = padded_2(rounded, (("gy", 0),), height)
    from_prev = along_cols(couple_y, padded[:height]).astype(jnp.bfloat16)
    from_next = along_cols_back(next_y, padded[2 * height :]).astype(jnp.bfloat16)
    from_prev = lax.optimization_barrier(from_prev)
    from_next = lax.optimization_barrier(from_next)
    return own + from_prev.astype(jnp.float32) + from_next.astype(jnp.float32)


def halo_body(noise, cheb_coeff, diag_x, couple_x, diag_y, couple_y, track_rows, track_obs, weights):
    next_x = shifted(couple_x, "gx", -1)
    next_y = shifted(couple_y, "gy", -1)

    def operator(field):
        return apply_cols(apply_rows(field, diag_x, couple_x, next_x), diag_y, couple_y, next_y)

    start = noise.astype(jnp.float32)
    terms = cheb_coeff.shape[0]
    previous = start
    current = operator(start)
    total = cheb_coeff[0] * start
    total = total + cheb_coeff[1] * current
    for term in range(2, terms):
        following = 2.0 * operator(current) - previous
        previous = current
        current = following
        total = total + cheb_coeff[term] * current
    height = total.shape[0]
    first_row = lax.axis_index("gy") * height
    local_rows = track_rows - first_row
    picked = jnp.take(total, local_rows, axis=0)
    misfit = picked - track_obs[:, :, None]
    piece = lax.all_gather(misfit.astype(jnp.bfloat16), "gy", axis=0, tiled=True).astype(
        jnp.float32
    )
    flat = piece.reshape(piece.shape[0], -1)
    correction = jnp.dot(
        weights, flat, precision=lax.Precision.HIGHEST, preferred_element_type=jnp.float32
    )
    return total - correction.reshape(total.shape)

LANES = 128
BF16 = jnp.bfloat16
F32 = jnp.float32


def halves(value):
    high = value.astype(BF16)
    return high, (value - high.astype(F32)).astype(BF16)


def offsets(count):
    return sorted(range(count), key=lambda k: -min(k, count - k))


def place(me, nx, ny, dx, dy):
    return (lax.rem(me[0] + dx, nx), lax.rem(me[1] + dy, ny))


def greet(nx, ny, me):
    barrier = pltpu.get_barrier_semaphore()
    for dx in range(nx):
        for dy in range(ny):
            if dx or dy:
                pl.semaphore_signal(barrier, inc=1, device_id=place(me, nx, ny, dx, dy))
    pl.semaphore_wait(barrier, nx * ny - 1)


def pack_kernel(tracks, rows_ref, noise_ref, dx_ref, kx_ref, dy_ref, ky_ref, obs_ref, w_ref, x_ref, px_ref, py_ref, buf):
    height, width, samples = noise_ref.shape
    lines = samples // 2
    low = lax.broadcasted_iota(jnp.int32, (lines, LANES), 1) < width

    def turn(q, _):
        both = noise_ref[pl.ds(2 * q, 2)].astype(F32).reshape(2 * width, samples)
        both = both.T
        first, second = both[:lines], both[lines:]
        one = jnp.where(low, first, pltpu.roll(second, width, 1))
        two = jnp.where(low, pltpu.roll(first, width, 1), second)
        buf[pl.ds(2 * q, lines, stride=height), :] = one
        buf[pl.ds(2 * q + 1, lines, stride=height), :] = two
        return 0

    lax.fori_loop(0, height // 2, turn, 0, unroll=4)

    def settle(p, _):
        x_ref[p] = buf[pl.ds(pl.multiple_of(p * height, height), height), :].astype(BF16)
        return 0

    lax.fori_loop(0, lines, settle, 0, unroll=8)
    px_ref[...] = jnp.concatenate([dx_ref[...], kx_ref[...].astype(F32)], axis=1).astype(BF16)
    py_ref[:height] = jnp.concatenate([dy_ref[...], ky_ref[...].astype(F32)], axis=1).astype(BF16)
    at = lax.axis_index("gy")
    per = rows_ref.shape[0]
    lane = lax.broadcasted_iota(jnp.int32, (height, tracks), 1)
    line = lax.broadcasted_iota(jnp.int32, (height, tracks), 0) + at * height
    hot = jnp.zeros((height, tracks), F32)
    for t in range(per):
        hot = hot + jnp.where((lane == at * per + t) & (line == rows_ref[t]), 1.0, 0.0)
    weight = w_ref[...]
    high = weight.astype(BF16).astype(F32)
    pad = jnp.zeros((height, LANES - 3 * tracks), F32)
    parts = [high, weight - high, hot] + ([pad] if pad.shape[1] else [])
    py_ref[height : 2 * height] = jnp.concatenate(parts, axis=1).astype(BF16)
    obs = obs_ref[...]
    top = obs.astype(BF16).astype(F32)
    obs = jnp.concatenate([top, obs - top], axis=1)
    if per % 16:
        obs = jnp.concatenate([obs, jnp.zeros((-per % 16, LANES), F32)], axis=0)
    py_ref[2 * height :] = obs.astype(BF16)


def unpack_kernel(per, y_ref, gys_ref, w_ref, out_ref, buf):
    lines, height, _ = y_ref.shape
    chunk, width, samples = out_ref.shape
    step = pl.program_id(0)

    @pl.when(step == 0)
    def _():
        ny = gys_ref.shape[0]
        seen = [gys_ref[c, 2 * height :].astype(F32)[:per] for c in range(ny)]
        seen = jnp.concatenate(seen, axis=0)
        seen = seen + pltpu.roll(seen, width, 1)
        level = jnp.dot(w_ref[...], seen, precision=lax.Precision.HIGHEST, preferred_element_type=F32)

        def spread(p, _):
            buf[pl.ds(pl.multiple_of(p * height, height), height), :] = y_ref[p].astype(F32) + level
            return 0

        lax.fori_loop(0, lines, spread, 0, unroll=8)

    low = lax.broadcasted_iota(jnp.int32, (width, LANES), 1) < lines

    def turn(q, _):
        row = step * chunk + 2 * q
        one = buf[pl.ds(row, lines, stride=height), :]
        two = buf[pl.ds(row + 1, lines, stride=height), :]
        both = jnp.concatenate([one, two], axis=0).T
        first, second = both[:width], both[width:]
        out_ref[2 * q] = jnp.where(low, first, pltpu.roll(second, lines, 1))
        out_ref[2 * q + 1] = jnp.where(low, pltpu.roll(first, lines, 1), second)
        return 0

    lax.fori_loop(0, chunk // 2, turn, 0, unroll=4)


def dot(a, b):
    return jnp.dot(a, b, preferred_element_type=F32)


def build_weights(nx, ny, width, tracks, gxs_ref, gys_ref, wx_ref, wy_ref, wp_ref):
    zero = jnp.zeros((width, width), F32)
    wx_ref[...] = jnp.zeros_like(wx_ref)
    wy_ref[...] = jnp.zeros_like(wy_ref)

    def put_x(out, inn, value):
        row = (inn - (out // 2 * 2 - 1)) * LANES
        lane = (out % 2) * LANES
        for half in range(2):
            sides = [value, zero] if half == 0 else [zero, value]
            wx_ref[out // 2, row + half * width : row + (half + 1) * width, lane : lane + LANES] = (
                jnp.concatenate(sides, axis=1).astype(BF16)
            )

    for b in range(nx):
        both = gxs_ref[b].astype(F32)
        turned = both.T
        put_x(b, b, turned[:width])
        if b:
            put_x(b, b - 1, turned[width:])
            put_x(b - 1, b, both[:, width:])
    blocks = [gys_ref[c, :width].astype(F32) for c in range(ny)]
    for c in range(ny):
        row = [zero] * ny
        row[c] = blocks[c][:, :width]
        if c:
            row[c - 1] = blocks[c][:, width:]
        if c < ny - 1:
            row[c + 1] = blocks[c + 1].T[width:]
        wy_ref[c * width : (c + 1) * width] = jnp.concatenate(row, axis=1).astype(BF16)
    extra = jnp.concatenate([gys_ref[c, width : 2 * width] for c in range(ny)], axis=0)
    hot = extra[:, 2 * tracks : 3 * tracks]
    for part in range(2):
        wp_ref[part] = lax.dot_general(
            extra[:, part * tracks : (part + 1) * tracks], hot, (((1,), (1,)), ((), ())),
            preferred_element_type=F32,
        ).astype(BF16)


def chebyshev(terms, wide, coeff_ref, wx_ref, wy_ref, wp_ref, cur, prev, total, u, cbf, ubf, emit):
    slab = 2 * LANES
    count = wide // slab
    cols = [slice(j * slab, (j + 1) * slab) for j in range(count)]

    def step(k, _):
        twice = jnp.where(k == 1, 1.0, 2.0)
        keep = jnp.where(k == 1, 0.0, 1.0)
        coeff = coeff_ref[k]
        for j in range(count):
            out = NUGGET * cur[:, cols[j]] + dot(cbf[:, j * slab : (j + 2) * slab], wx_ref[j])
            u[:, cols[j]] = out
            ubf[:, cols[j]] = out.astype(BF16)
        for j in range(count):
            out = NUGGET * u[:, cols[j]] + dot(wy_ref[...], ubf[:, cols[j]])
            old = cur[:, cols[j]]
            new = twice * out - keep * prev[:, cols[j]]
            prev[:, cols[j]] = old
            cur[:, cols[j]] = new
            total[:, cols[j]] += coeff * new
            cbf[:, LANES + j * slab : LANES + (j + 1) * slab] = new.astype(BF16)
        return 0

    lax.fori_loop(1, terms, step, 0)
    for j in range(count):
        field = total[:, cols[j]]
        high, low = halves(field)
        fix = dot(wp_ref[0], high) + dot(wp_ref[0], low) + dot(wp_ref[1], high)
        emit(cols[j], field - fix)


def main_kernel(nx, ny, width, tracks, coeff_ref, x_ref, gx_ref, gy_ref, y_ref, gys_ref, v_ref, out_ref, gxs_ref,
                wx_ref, wy_ref, wp_ref, cur, prev, total, u, cbf, ubf,
                local, send, recv, back, home, xsend, xrecv, ysend, yrecv):
    me = (lax.axis_index("gx"), lax.axis_index("gy"))
    pairs, tall, wide = v_ref.shape
    height = tall // ny

    def line(at, pair):
        return (at[0] * ny + at[1]) * pairs + pair

    def tile(ref, at, pair):
        return ref.at[pair, pl.ds(pl.multiple_of(at[1] * height, height), height), pl.ds(pl.multiple_of(at[0] * LANES, LANES), LANES)]

    own = [pltpu.make_async_copy(x_ref.at[line(me, pair)], tile(v_ref, me, pair), local.at[pair]) for pair in range(pairs)]
    own.append(pltpu.make_async_copy(gx_ref, gxs_ref.at[me[0]], local.at[pairs]))
    own.append(pltpu.make_async_copy(gy_ref, gys_ref.at[me[1]], local.at[pairs + 1]))
    for copy in own:
        copy.start()
    greet(nx, ny, me)

    def block(dx, dy, pair, at):
        to = place(me, nx, ny, dx, dy)
        return pltpu.make_async_remote_copy(
            src_ref=x_ref.at[line(to, pair)], dst_ref=tile(v_ref, at, pair),
            send_sem=send.at[pair, dx * ny + dy], recv_sem=recv.at[pair, dx * ny + dy], device_id=to,
        )

    def result(dx, dy, pair, at):
        to = place(me, nx, ny, dx, dy)
        return pltpu.make_async_remote_copy(
            src_ref=tile(out_ref, to, pair), dst_ref=y_ref.at[line(at, pair)],
            send_sem=back.at[pair, dx * ny + dy], recv_sem=home.at[pair, dx * ny + dy], device_id=to,
        )

    def part_x(dx, at):
        return pltpu.make_async_remote_copy(
            src_ref=gx_ref, dst_ref=gxs_ref.at[at[0]], send_sem=xsend.at[dx], recv_sem=xrecv.at[dx],
            device_id=place(me, nx, ny, dx, 0),
        )

    def part_y(dy, at):
        return pltpu.make_async_remote_copy(
            src_ref=gy_ref, dst_ref=gys_ref.at[at[1]], send_sem=ysend.at[dy], recv_sem=yrecv.at[dy],
            device_id=place(me, nx, ny, 0, dy),
        )

    order = [(dx, dy) for dx in offsets(nx) for dy in offsets(ny) if dx or dy]
    for dx in offsets(nx):
        if dx:
            part_x(dx, me).start()
    for dy in offsets(ny):
        if dy:
            part_y(dy, me).start()
    for pair in range(pairs):
        for dx, dy in order:
            block(dx, dy, pair, me).start()
    own[pairs].wait()
    own[pairs + 1].wait()
    for dx in offsets(nx):
        if dx:
            part_x(dx, place(me, nx, ny, nx - dx, 0)).wait()
    for dy in offsets(ny):
        if dy:
            part_y(dy, place(me, nx, ny, 0, ny - dy)).wait()
    build_weights(nx, ny, width, tracks, gxs_ref, gys_ref, wx_ref, wy_ref, wp_ref)
    cbf[:, :LANES] = jnp.zeros((tall, LANES), BF16)
    cbf[:, LANES + wide :] = jnp.zeros((tall, LANES), BF16)
    mine = []
    for pair in range(pairs):
        own[pair].wait()
        for dx, dy in order:
            block(dx, dy, pair, place(me, nx, ny, nx - dx, ny - dy)).wait()
        value = v_ref[pair]
        cbf[:, LANES : LANES + wide] = value
        start = value.astype(F32)
        cur[...] = start
        prev[...] = start
        total[...] = coeff_ref[0] * start

        def emit(col, value, pair=pair):
            out_ref[pair, :, col] = value.astype(BF16)

        chebyshev(coeff_ref.shape[0], wide, coeff_ref, wx_ref, wy_ref, wp_ref, cur, prev, total, u, cbf, ubf, emit)
        for dx, dy in order:
            result(dx, dy, pair, me).start()
        mine.append(pltpu.make_async_copy(tile(out_ref, me, pair), y_ref.at[line(me, pair)], local.at[pair]))
        mine[-1].start()
    for pair in range(pairs):
        for dx, dy in order:
            result(dx, dy, pair, place(me, nx, ny, nx - dx, ny - dy)).wait()
        mine[pair].wait()


def swap_body(nx, ny, noise, cheb_coeff, diag_x, couple_x, diag_y, couple_y, track_rows, track_obs, weights):
    height, width, samples = noise.shape
    tracks = weights.shape[1]
    per = track_rows.shape[0]
    lines = samples // 2
    devices = nx * ny
    pairs = lines // devices
    tall, wide = ny * height, nx * LANES
    rows = 2 * height + per + -per % 16
    vmem = pl.BlockSpec(memory_space=pltpu.VMEM)
    smem = pl.BlockSpec(memory_space=pltpu.SMEM)
    dma = pltpu.SemaphoreType.DMA
    mixed = pltpu.VMEM((lines * height, LANES), F32)
    x, part_x, part_y = pl.pallas_call(
        lambda *refs: pack_kernel(tracks, *refs),
        out_shape=(
            jax.ShapeDtypeStruct((lines, height, LANES), BF16),
            jax.ShapeDtypeStruct((width, LANES), BF16),
            jax.ShapeDtypeStruct((rows, LANES), BF16),
        ),
        in_specs=[smem] + [vmem] * 7,
        out_specs=(vmem,) * 3,
        scratch_shapes=[mixed],
        name="pack",
    )(track_rows, noise, diag_x, couple_x, diag_y, couple_y, track_obs, weights)
    field = pltpu.VMEM((tall, wide), F32)
    half = pltpu.VMEM((pairs, tall, wide), BF16)
    y, gys = pl.pallas_call(
        lambda *refs: main_kernel(nx, ny, width, tracks, *refs),
        out_shape=(
            jax.ShapeDtypeStruct((lines, height, LANES), BF16),
            jax.ShapeDtypeStruct((ny, rows, LANES), BF16),
        ),
        in_specs=[smem, vmem, vmem, vmem],
        out_specs=(vmem, vmem),
        scratch_shapes=[
            half, half,
            pltpu.VMEM((nx, width, LANES), BF16),
            pltpu.VMEM((nx // 2, 4 * LANES, 2 * LANES), BF16),
            pltpu.VMEM((tall, tall), BF16),
            pltpu.VMEM((2, tall, tall), BF16),
            field, field, field, field,
            pltpu.VMEM((tall, wide + 2 * LANES), BF16),
            pltpu.VMEM((tall, wide), BF16),
            dma((pairs + 2,)),
            dma((pairs, devices)), dma((pairs, devices)), dma((pairs, devices)), dma((pairs, devices)),
            dma((nx,)), dma((nx,)), dma((ny,)), dma((ny,)),
        ],
        compiler_params=pltpu.CompilerParams(collective_id=0, has_side_effects=True),
        name="swap",
    )(cheb_coeff, x, part_x, part_y)
    chunk = height // 4
    return pl.pallas_call(
        lambda *refs: unpack_kernel(per, *refs),
        grid=(height // chunk,),
        out_shape=jax.ShapeDtypeStruct((height, width, samples), F32),
        in_specs=[vmem, vmem, vmem],
        out_specs=pl.BlockSpec((chunk, width, samples), lambda i: (i, 0, 0)),
        scratch_shapes=[mixed],
        name="unpack",
    )(y, gys, weights)


def body(noise, *rest):
    nx, ny = lax.axis_size("gx"), lax.axis_size("gy")
    height, width, samples = noise.shape
    tracks, per = rest[-1].shape[1], rest[-3].shape[0]
    fits = 2 * width == LANES and height == width and nx % 2 == 0 and samples % (2 * nx * ny) == 0 and samples == LANES
    fits = fits and 3 * tracks <= LANES and per * ny == tracks
    if fits:
        return swap_body(nx, ny, noise, *rest)
    return halo_body(noise, *rest)


def solution(mesh):
    return jax.shard_map(
        body,
        mesh=mesh,
        in_specs=(
            P("gy", "gx", None),
            P(),
            P("gx", None),
            P("gx", None),
            P("gy", None),
            P("gy", None),
            P("gy"),
            P("gy", "gx"),
            P("gy", None),
        ),
        out_specs=P("gy", "gx", None),
        check_vma=False,
    )
```

```python
import jax
import jax.numpy as jnp
from jax import lax
from jax.experimental import pallas as pl
from jax.experimental.pallas import tpu as pltpu
from jax.sharding import PartitionSpec as P

NUGGET = 0.3


def padded_2(value, sides, width):
    for axis, dim in sides:
        size, length = (lax.axis_size(axis), value.shape[dim])
        up = [(i, (i + 1) % size) for i in range(size - 1)]
        down = [(j, i) for i, j in up]
        last = lax.slice_in_dim(value, length - width, length, axis=dim)
        leading = lax.slice_in_dim(value, 0, width, axis=dim)
        before = lax.ppermute(last, axis, up)
        after = lax.ppermute(leading, axis, down)
        value = jnp.concatenate([before, value, after], axis=dim)
    return value


def shifted(value, axis, steps):
    count = lax.axis_size(axis)
    leading, last = (max(0, -steps), min(count, count - steps))
    return lax.ppermute(value, axis, [(source, source + steps) for source in range(leading, last)])


def along_rows(matrix, field):
    return jnp.einsum("ij,yjs->yis", matrix, field, preferred_element_type=jnp.float32)


def along_rows_back(matrix, field):
    return jnp.einsum("ji,yjs->yis", matrix, field, preferred_element_type=jnp.float32)


def along_cols(matrix, field):
    flat = field.reshape(field.shape[0], -1)
    return jnp.dot(matrix, flat, preferred_element_type=jnp.float32).reshape(field.shape)


def along_cols_back(matrix, field):
    flat = field.reshape(field.shape[0], -1)
    return jnp.dot(matrix.T, flat, preferred_element_type=jnp.float32).reshape(field.shape)


def apply_rows(field, diag_x, couple_x, next_x):
    width = field.shape[1]
    own = NUGGET * field + jnp.einsum(
        "ij,yjs->yis",
        diag_x,
        field,
        precision=lax.Precision.HIGHEST,
        preferred_element_type=jnp.float32,
    )
    rounded = field.astype(jnp.bfloat16)
    padded = padded_2(rounded, (("gx", 1),), width)
    from_prev = along_rows(couple_x, padded[:, :width]).astype(jnp.bfloat16)
    from_next = along_rows_back(next_x, padded[:, 2 * width :]).astype(jnp.bfloat16)
    from_prev = lax.optimization_barrier(from_prev)
    from_next = lax.optimization_barrier(from_next)
    return own + from_prev.astype(jnp.float32) + from_next.astype(jnp.float32)


def apply_cols(field, diag_y, couple_y, next_y):
    height = field.shape[0]
    own = NUGGET * field + jnp.dot(
        diag_y,
        field.reshape(height, -1),
        precision=lax.Precision.HIGHEST,
        preferred_element_type=jnp.float32,
    ).reshape(field.shape)
    rounded = field.astype(jnp.bfloat16)
    padded = padded_2(rounded, (("gy", 0),), height)
    from_prev = along_cols(couple_y, padded[:height]).astype(jnp.bfloat16)
    from_next = along_cols_back(next_y, padded[2 * height :]).astype(jnp.bfloat16)
    from_prev = lax.optimization_barrier(from_prev)
    from_next = lax.optimization_barrier(from_next)
    return own + from_prev.astype(jnp.float32) + from_next.astype(jnp.float32)


def halo_body(noise, cheb_coeff, diag_x, couple_x, diag_y, couple_y, track_rows, track_obs, weights):
    next_x = shifted(couple_x, "gx", -1)
    next_y = shifted(couple_y, "gy", -1)

    def operator(field):
        return apply_cols(apply_rows(field, diag_x, couple_x, next_x), diag_y, couple_y, next_y)

    start = noise.astype(jnp.float32)
    terms = cheb_coeff.shape[0]
    previous = start
    current = operator(start)
    total = cheb_coeff[0] * start
    total = total + cheb_coeff[1] * current
    for term in range(2, terms):
        following = 2.0 * operator(current) - previous
        previous = current
        current = following
        total = total + cheb_coeff[term] * current
    height = total.shape[0]
    first_row = lax.axis_index("gy") * height
    local_rows = track_rows - first_row
    picked = jnp.take(total, local_rows, axis=0)
    misfit = picked - track_obs[:, :, None]
    piece = lax.all_gather(misfit.astype(jnp.bfloat16), "gy", axis=0, tiled=True).astype(
        jnp.float32
    )
    flat = piece.reshape(piece.shape[0], -1)
    correction = jnp.dot(
        weights, flat, precision=lax.Precision.HIGHEST, preferred_element_type=jnp.float32
    )
    return total - correction.reshape(total.shape)

LANES = 128
BF16 = jnp.bfloat16
F32 = jnp.float32


def halves(value):
    high = value.astype(BF16)
    return high, (value - high.astype(F32)).astype(BF16)


def offsets(count):
    return sorted(range(count), key=lambda k: -min(k, count - k))


def place(me, nx, ny, dx, dy):
    return (lax.rem(me[0] + dx, nx), lax.rem(me[1] + dy, ny))


PAD = 8


def greet(nx, ny, me):
    barrier = pltpu.get_barrier_semaphore()
    for dx in range(nx):
        for dy in range(ny):
            if dx or dy:
                pl.semaphore_signal(barrier, inc=1, device_id=place(me, nx, ny, dx, dy))


def turn_rows(first, count, noise_ref, x_ref, buf):
    height, width, samples = noise_ref.shape
    lines = samples // 2
    low = lax.broadcasted_iota(jnp.int32, (lines, LANES), 1) < width

    def turn(q, _):
        row = first + 2 * q
        both = noise_ref[pl.ds(row, 2)].astype(F32).reshape(2 * width, samples)
        both = both.T
        upper, lower = both[:lines], both[lines:]
        one = jnp.where(low, upper, pltpu.roll(lower, width, 1))
        two = jnp.where(low, pltpu.roll(upper, width, 1), lower)
        buf[pl.ds(row, lines, stride=height + PAD), :] = one
        buf[pl.ds(row + 1, lines, stride=height + PAD), :] = two
        return 0

    lax.fori_loop(0, count // 2, turn, 0, unroll=4)

    def settle(p, _):
        start = pl.multiple_of(p * (height + PAD) + first, 8)
        x_ref[p, first : first + count] = buf[pl.ds(start, count), :].astype(BF16)
        return 0

    lax.fori_loop(0, lines, settle, 0, unroll=8)


def pack_small(tracks, height, rows_ref, dx_ref, kx_ref, dy_ref, ky_ref, obs_ref, w_ref, px_ref, py_ref):
    px_ref[...] = jnp.concatenate([dx_ref[...], kx_ref[...].astype(F32)], axis=1).astype(BF16)
    py_ref[:height] = jnp.concatenate([dy_ref[...], ky_ref[...].astype(F32)], axis=1).astype(BF16)
    at = lax.axis_index("gy")
    per = rows_ref.shape[0]
    lane = lax.broadcasted_iota(jnp.int32, (height, tracks), 1)
    line = lax.broadcasted_iota(jnp.int32, (height, tracks), 0) + at * height
    hot = jnp.zeros((height, tracks), F32)
    for t in range(per):
        hot = hot + jnp.where((lane == at * per + t) & (line == rows_ref[t]), 1.0, 0.0)
    weight = w_ref[...].T
    high = weight.astype(BF16).astype(F32)
    pad = jnp.zeros((height, LANES - 3 * tracks), F32)
    parts = [high, weight - high, hot] + ([pad] if pad.shape[1] else [])
    py_ref[height : 2 * height] = jnp.concatenate(parts, axis=1).astype(BF16)
    obs = obs_ref[...]
    top = obs.astype(BF16).astype(F32)
    obs = jnp.concatenate([top, obs - top], axis=1)
    if per % 16:
        obs = jnp.concatenate([obs, jnp.zeros((-per % 16, LANES), F32)], axis=0)
    py_ref[2 * height :] = obs.astype(BF16)


def unpack_kernel(per, y_ref, gys_ref, w_ref, out_ref, buf):
    lines, height, _ = y_ref.shape
    chunk, width, samples = out_ref.shape
    step = pl.program_id(0)

    @pl.when(step == 0)
    def _():
        ny = gys_ref.shape[0]
        seen = [gys_ref[c, 2 * height :].astype(F32)[:per] for c in range(ny)]
        seen = jnp.concatenate(seen, axis=0)
        seen = seen + pltpu.roll(seen, width, 1)
        level = lax.dot_general(
            w_ref[...], seen, (((0,), (0,)), ((), ())), precision=lax.Precision.HIGHEST, preferred_element_type=F32
        )

        def spread(p, _):
            buf[pl.ds(pl.multiple_of(p * (height + PAD), 8), height), :] = y_ref[p].astype(F32) + level
            return 0

        lax.fori_loop(0, lines, spread, 0, unroll=8)

    low = lax.broadcasted_iota(jnp.int32, (width, LANES), 1) < lines

    def turn(q, _):
        row = step * chunk + 2 * q
        one = buf[pl.ds(row, lines, stride=height + PAD), :]
        two = buf[pl.ds(row + 1, lines, stride=height + PAD), :]
        both = jnp.concatenate([one, two], axis=0).T
        first, second = both[:width], both[width:]
        out_ref[2 * q] = jnp.where(low, first, pltpu.roll(second, lines, 1))
        out_ref[2 * q + 1] = jnp.where(low, pltpu.roll(first, lines, 1), second)
        return 0

    lax.fori_loop(0, chunk // 2, turn, 0, unroll=4)


def dot(a, b):
    return jnp.dot(a, b, preferred_element_type=F32)


def build_weights(nx, ny, width, tracks, gxs_ref, gys_ref, wx_ref, wy_ref, wp_ref):
    zero = jnp.zeros((width, width), F32)
    wx_ref[...] = jnp.zeros_like(wx_ref)
    wy_ref[...] = jnp.zeros_like(wy_ref)

    def put_x(out, inn, value):
        row = (inn - (out // 2 * 2 - 1)) * LANES
        lane = (out % 2) * LANES
        for half in range(2):
            sides = [value, zero] if half == 0 else [zero, value]
            wx_ref[out // 2, row + half * width : row + (half + 1) * width, lane : lane + LANES] = (
                jnp.concatenate(sides, axis=1).astype(BF16)
            )

    for b in range(nx):
        both = gxs_ref[b].astype(F32)
        turned = both.T
        put_x(b, b, turned[:width])
        if b:
            put_x(b, b - 1, turned[width:])
            put_x(b - 1, b, both[:, width:])
    blocks = [gys_ref[c, :width].astype(F32) for c in range(ny)]
    for c in range(ny):
        row = [zero] * ny
        row[c] = blocks[c][:, :width]
        if c:
            row[c - 1] = blocks[c][:, width:]
        if c < ny - 1:
            row[c + 1] = blocks[c + 1].T[width:]
        wy_ref[c * width : (c + 1) * width] = jnp.concatenate(row, axis=1).astype(BF16)
    extra = jnp.concatenate([gys_ref[c, width : 2 * width] for c in range(ny)], axis=0)
    hot = extra[:, 2 * tracks : 3 * tracks]
    for part in range(2):
        wp_ref[part] = lax.dot_general(
            extra[:, part * tracks : (part + 1) * tracks], hot, (((1,), (1,)), ((), ())),
            preferred_element_type=F32,
        ).astype(BF16)


def chebyshev(terms, wide, coeff_ref, wx_ref, wy_ref, wp_ref, cur, prev, total, u, cbf, ubf, emit):
    slab = 2 * LANES
    count = wide // slab
    cols = [slice(j * slab, (j + 1) * slab) for j in range(count)]

    def step(k, _):
        twice = jnp.where(k == 1, 1.0, 2.0)
        keep = jnp.where(k == 1, 0.0, 1.0)
        coeff = coeff_ref[k]
        for j in range(count):
            out = NUGGET * cur[:, cols[j]] + dot(cbf[:, j * slab : (j + 2) * slab], wx_ref[j])
            u[:, cols[j]] = out
            ubf[:, cols[j]] = out.astype(BF16)
        for j in range(count):
            out = NUGGET * u[:, cols[j]] + dot(wy_ref[...], ubf[:, cols[j]])
            old = cur[:, cols[j]]
            new = twice * out - keep * prev[:, cols[j]]
            prev[:, cols[j]] = old
            cur[:, cols[j]] = new
            total[:, cols[j]] += coeff * new
            cbf[:, LANES + j * slab : LANES + (j + 1) * slab] = new.astype(BF16)
        return 0

    lax.fori_loop(1, terms, step, 0)
    for j in range(count):
        field = total[:, cols[j]]
        high, low = halves(field)
        fix = dot(wp_ref[0], high) + dot(wp_ref[0], low) + dot(wp_ref[1], high)
        emit(cols[j], field - fix)


def main_kernel(nx, ny, width, tracks, rows_ref, coeff_ref, noise_hbm, dx_ref, kx_ref, dy_ref, ky_ref, obs_ref, w_ref,
                y_ref, gys_ref, noise_ref, buf, x_ref, gx_ref, gy_ref, v_ref, out_ref, gxs_ref, wx_ref, wy_ref, wp_ref, cur, prev, total, u, cbf, ubf,
                load, local, send, recv, early, first, back, home, xsend, xrecv, fsend, frecv, ysend, yrecv):
    me = (lax.axis_index("gx"), lax.axis_index("gy"))
    pairs, tall, wide = v_ref.shape
    height = tall // ny

    def line(at, pair):
        return (at[0] * ny + at[1]) * pairs + pair

    def tile(ref, at, pair):
        return ref.at[pair, pl.ds(pl.multiple_of(at[1] * height, height), height), pl.ds(pl.multiple_of(at[0] * LANES, LANES), LANES)]

    half = height // 2
    quarter = width // ny
    loads = []
    for part in range(2):
        rows = pl.ds(part * half, half)
        loads.append(pltpu.make_async_copy(noise_hbm.at[rows], noise_ref.at[rows], load.at[part]))
        loads[part].start()
    greet(nx, ny, me)
    pack_small(tracks, height, rows_ref, dx_ref, kx_ref, dy_ref, ky_ref, obs_ref, w_ref, gx_ref, gy_ref)
    loads[0].wait()
    turn_rows(0, half, noise_ref, x_ref, buf)
    pl.semaphore_wait(pltpu.get_barrier_semaphore(), nx * ny - 1)
    slot = pl.ds(pl.multiple_of(me[1] * quarter, quarter), quarter)

    def piece(dx, dy, at):
        to = place(me, nx, ny, dx, dy)
        start = pl.multiple_of(at[1] * height, height)
        return pltpu.make_async_remote_copy(
            src_ref=x_ref.at[line(to, 0), pl.ds(0, half)],
            dst_ref=v_ref.at[0, pl.ds(start, half), pl.ds(pl.multiple_of(at[0] * LANES, LANES), LANES)],
            send_sem=early.at[dx * ny + dy], recv_sem=first.at[dx * ny + dy], device_id=to,
        )

    def block(dx, dy, pair, at):
        to = place(me, nx, ny, dx, dy)
        source, target = x_ref.at[line(to, pair)], tile(v_ref, at, pair)
        if pair == 0:
            start = pl.multiple_of(at[1] * height + half, half)
            source = x_ref.at[line(to, 0), pl.ds(half, half)]
            target = v_ref.at[0, pl.ds(start, half), pl.ds(pl.multiple_of(at[0] * LANES, LANES), LANES)]
        return pltpu.make_async_remote_copy(
            src_ref=source, dst_ref=target,
            send_sem=send.at[pair, dx * ny + dy], recv_sem=recv.at[pair, dx * ny + dy], device_id=to,
        )

    def result(dx, dy, pair, at):
        to = place(me, nx, ny, dx, dy)
        return pltpu.make_async_remote_copy(
            src_ref=tile(out_ref, to, pair), dst_ref=y_ref.at[line(at, pair)],
            send_sem=back.at[pair, dx * ny + dy], recv_sem=home.at[pair, dx * ny + dy], device_id=to,
        )

    def part_x(dx, at):
        return pltpu.make_async_remote_copy(
            src_ref=gx_ref.at[slot], dst_ref=gxs_ref.at[at[0], slot], send_sem=xsend.at[dx], recv_sem=xrecv.at[dx],
            device_id=place(me, nx, ny, dx, 0),
        )

    def part_y(dy, at):
        return pltpu.make_async_remote_copy(
            src_ref=gy_ref, dst_ref=gys_ref.at[at[1]], send_sem=ysend.at[dy], recv_sem=yrecv.at[dy],
            device_id=place(me, nx, ny, 0, dy),
        )

    def spread_x(dy, at):
        spot = pl.ds(pl.multiple_of(at[1] * quarter, quarter), quarter)
        return pltpu.make_async_remote_copy(
            src_ref=gxs_ref.at[:, spot], dst_ref=gxs_ref.at[:, spot], send_sem=fsend.at[dy], recv_sem=frecv.at[dy],
            device_id=place(me, nx, ny, 0, dy),
        )

    order = [(dx, dy) for dx in offsets(nx) for dy in offsets(ny) if dx or dy]
    for dx in offsets(nx):
        if dx:
            part_x(dx, me).start()
    for dx, dy in order:
        piece(dx, dy, me).start()
    for dy in offsets(ny):
        if dy:
            part_y(dy, me).start()
    own = [
        pltpu.make_async_copy(gx_ref.at[slot], gxs_ref.at[me[0], slot], local.at[0]),
        pltpu.make_async_copy(gy_ref, gys_ref.at[me[1]], local.at[1]),
    ]
    for copy in own:
        copy.start()
    loads[1].wait()
    turn_rows(half, half, noise_ref, x_ref, buf)
    for pair in range(pairs):
        for dx, dy in order:
            block(dx, dy, pair, me).start()
        own.append(pltpu.make_async_copy(x_ref.at[line(me, pair)], tile(v_ref, me, pair), local.at[2 + pair]))
        own[-1].start()
    own[0].wait()
    own[1].wait()
    for dx in offsets(nx):
        if dx:
            part_x(dx, place(me, nx, ny, nx - dx, 0)).wait()
    for dy in offsets(ny):
        if dy:
            spread_x(dy, me).start()
    for dy in offsets(ny):
        if dy:
            part_y(dy, place(me, nx, ny, 0, ny - dy)).wait()
    for dy in offsets(ny):
        if dy:
            spread_x(dy, me).wait_send()
            spread_x(dy, place(me, nx, ny, 0, ny - dy)).wait_recv()
    build_weights(nx, ny, width, tracks, gxs_ref, gys_ref, wx_ref, wy_ref, wp_ref)
    cbf[:, :LANES] = jnp.zeros((tall, LANES), BF16)
    cbf[:, LANES + wide :] = jnp.zeros((tall, LANES), BF16)
    mine = []
    for pair in range(pairs):
        own[2 + pair].wait()
        if pair == 0:
            for dx, dy in order:
                piece(dx, dy, place(me, nx, ny, nx - dx, ny - dy)).wait()
        for dx, dy in order:
            block(dx, dy, pair, place(me, nx, ny, nx - dx, ny - dy)).wait()
        value = v_ref[pair]
        cbf[:, LANES : LANES + wide] = value
        start = value.astype(F32)
        cur[...] = start
        prev[...] = start
        total[...] = coeff_ref[0] * start

        def emit(col, value, pair=pair):
            out_ref[pair, :, col] = value.astype(BF16)

        chebyshev(coeff_ref.shape[0], wide, coeff_ref, wx_ref, wy_ref, wp_ref, cur, prev, total, u, cbf, ubf, emit)
        for dx, dy in order:
            result(dx, dy, pair, me).start()
        mine.append(pltpu.make_async_copy(tile(out_ref, me, pair), y_ref.at[line(me, pair)], local.at[2 + pair]))
        mine[-1].start()
    for pair in range(pairs):
        for dx, dy in order:
            result(dx, dy, pair, place(me, nx, ny, nx - dx, ny - dy)).wait()
        mine[pair].wait()


def swap_body(nx, ny, noise, cheb_coeff, diag_x, couple_x, diag_y, couple_y, track_rows, track_obs, weights):
    height, width, samples = noise.shape
    tracks = weights.shape[1]
    per = track_rows.shape[0]
    lines = samples // 2
    devices = nx * ny
    pairs = lines // devices
    tall, wide = ny * height, nx * LANES
    rows = 2 * height + per + -per % 16
    vmem = pl.BlockSpec(memory_space=pltpu.VMEM)
    smem = pl.BlockSpec(memory_space=pltpu.SMEM)
    dma = pltpu.SemaphoreType.DMA
    mixed = pltpu.VMEM((lines * (height + PAD), LANES), F32)
    field = pltpu.VMEM((tall, wide), F32)
    half = pltpu.VMEM((pairs, tall, wide), BF16)
    y, gys = pl.pallas_call(
        lambda *refs: main_kernel(nx, ny, width, tracks, *refs),
        out_shape=(
            jax.ShapeDtypeStruct((lines, height, LANES), BF16),
            jax.ShapeDtypeStruct((ny, rows, LANES), BF16),
        ),
        in_specs=[smem, smem, pl.BlockSpec(memory_space=pl.ANY)] + [vmem] * 6,
        out_specs=(vmem, vmem),
        scratch_shapes=[
            pltpu.VMEM((height, width, samples), BF16),
            mixed,
            pltpu.VMEM((lines, height, LANES), BF16),
            pltpu.VMEM((width, LANES), BF16),
            pltpu.VMEM((rows, LANES), BF16),
            half, half,
            pltpu.VMEM((nx, width, LANES), BF16),
            pltpu.VMEM((nx // 2, 4 * LANES, 2 * LANES), BF16),
            pltpu.VMEM((tall, tall), BF16),
            pltpu.VMEM((2, tall, tall), BF16),
            field, field, field, field,
            pltpu.VMEM((tall, wide + 2 * LANES), BF16),
            pltpu.VMEM((tall, wide), BF16),
            dma((2,)), dma((pairs + 2,)),
            dma((pairs, devices)), dma((pairs, devices)), dma((devices,)), dma((devices,)),
            dma((pairs, devices)), dma((pairs, devices)),
            dma((nx,)), dma((nx,)), dma((ny,)), dma((ny,)), dma((ny,)), dma((ny,)),
        ],
        compiler_params=pltpu.CompilerParams(collective_id=0, has_side_effects=True),
        name="swap",
    )(track_rows, cheb_coeff, noise, diag_x, couple_x, diag_y, couple_y, track_obs, weights.T)
    chunk = height // 4
    return pl.pallas_call(
        lambda *refs: unpack_kernel(per, *refs),
        grid=(height // chunk,),
        out_shape=jax.ShapeDtypeStruct((height, width, samples), F32),
        in_specs=[vmem, vmem, vmem],
        out_specs=pl.BlockSpec((chunk, width, samples), lambda i: (i, 0, 0)),
        scratch_shapes=[mixed],
        name="unpack",
    )(y, gys, weights.T)


def body(noise, *rest):
    nx, ny = lax.axis_size("gx"), lax.axis_size("gy")
    height, width, samples = noise.shape
    tracks, per = rest[-1].shape[1], rest[-3].shape[0]
    fits = 2 * width == LANES and height == width and nx % 2 == 0 and samples % (2 * nx * ny) == 0 and samples == LANES
    fits = fits and width % (16 * ny) == 0 and 3 * tracks <= LANES and per * ny == tracks
    if fits:
        return swap_body(nx, ny, noise, *rest)
    return halo_body(noise, *rest)


def solution(mesh):
    return jax.shard_map(
        body,
        mesh=mesh,
        in_specs=(
            P("gy", "gx", None),
            P(),
            P("gx", None),
            P("gx", None),
            P("gy", None),
            P("gy", None),
            P("gy"),
            P("gy", "gx"),
            P("gy", None),
        ),
        out_specs=P("gy", "gx", None),
        check_vma=False,
    )
```

```python
import jax
import jax.numpy as jnp
from jax import lax
from jax.experimental import pallas as pl
from jax.experimental.pallas import tpu as pltpu
from jax.sharding import PartitionSpec as P

NUGGET = 0.3


def padded_2(value, sides, width):
    for axis, dim in sides:
        size, length = (lax.axis_size(axis), value.shape[dim])
        up = [(i, (i + 1) % size) for i in range(size - 1)]
        down = [(j, i) for i, j in up]
        last = lax.slice_in_dim(value, length - width, length, axis=dim)
        leading = lax.slice_in_dim(value, 0, width, axis=dim)
        before = lax.ppermute(last, axis, up)
        after = lax.ppermute(leading, axis, down)
        value = jnp.concatenate([before, value, after], axis=dim)
    return value


def shifted(value, axis, steps):
    count = lax.axis_size(axis)
    leading, last = (max(0, -steps), min(count, count - steps))
    return lax.ppermute(value, axis, [(source, source + steps) for source in range(leading, last)])


def along_rows(matrix, field):
    return jnp.einsum("ij,yjs->yis", matrix, field, preferred_element_type=jnp.float32)


def along_rows_back(matrix, field):
    return jnp.einsum("ji,yjs->yis", matrix, field, preferred_element_type=jnp.float32)


def along_cols(matrix, field):
    flat = field.reshape(field.shape[0], -1)
    return jnp.dot(matrix, flat, preferred_element_type=jnp.float32).reshape(field.shape)


def along_cols_back(matrix, field):
    flat = field.reshape(field.shape[0], -1)
    return jnp.dot(matrix.T, flat, preferred_element_type=jnp.float32).reshape(field.shape)


def apply_rows(field, diag_x, couple_x, next_x):
    width = field.shape[1]
    own = NUGGET * field + jnp.einsum(
        "ij,yjs->yis",
        diag_x,
        field,
        precision=lax.Precision.HIGHEST,
        preferred_element_type=jnp.float32,
    )
    rounded = field.astype(jnp.bfloat16)
    padded = padded_2(rounded, (("gx", 1),), width)
    from_prev = along_rows(couple_x, padded[:, :width]).astype(jnp.bfloat16)
    from_next = along_rows_back(next_x, padded[:, 2 * width :]).astype(jnp.bfloat16)
    from_prev = lax.optimization_barrier(from_prev)
    from_next = lax.optimization_barrier(from_next)
    return own + from_prev.astype(jnp.float32) + from_next.astype(jnp.float32)


def apply_cols(field, diag_y, couple_y, next_y):
    height = field.shape[0]
    own = NUGGET * field + jnp.dot(
        diag_y,
        field.reshape(height, -1),
        precision=lax.Precision.HIGHEST,
        preferred_element_type=jnp.float32,
    ).reshape(field.shape)
    rounded = field.astype(jnp.bfloat16)
    padded = padded_2(rounded, (("gy", 0),), height)
    from_prev = along_cols(couple_y, padded[:height]).astype(jnp.bfloat16)
    from_next = along_cols_back(next_y, padded[2 * height :]).astype(jnp.bfloat16)
    from_prev = lax.optimization_barrier(from_prev)
    from_next = lax.optimization_barrier(from_next)
    return own + from_prev.astype(jnp.float32) + from_next.astype(jnp.float32)


def halo_body(noise, cheb_coeff, diag_x, couple_x, diag_y, couple_y, track_rows, track_obs, weights):
    next_x = shifted(couple_x, "gx", -1)
    next_y = shifted(couple_y, "gy", -1)

    def operator(field):
        return apply_cols(apply_rows(field, diag_x, couple_x, next_x), diag_y, couple_y, next_y)

    start = noise.astype(jnp.float32)
    terms = cheb_coeff.shape[0]
    previous = start
    current = operator(start)
    total = cheb_coeff[0] * start
    total = total + cheb_coeff[1] * current
    for term in range(2, terms):
        following = 2.0 * operator(current) - previous
        previous = current
        current = following
        total = total + cheb_coeff[term] * current
    height = total.shape[0]
    first_row = lax.axis_index("gy") * height
    local_rows = track_rows - first_row
    picked = jnp.take(total, local_rows, axis=0)
    misfit = picked - track_obs[:, :, None]
    piece = lax.all_gather(misfit.astype(jnp.bfloat16), "gy", axis=0, tiled=True).astype(
        jnp.float32
    )
    flat = piece.reshape(piece.shape[0], -1)
    correction = jnp.dot(
        weights, flat, precision=lax.Precision.HIGHEST, preferred_element_type=jnp.float32
    )
    return total - correction.reshape(total.shape)

LANES = 128
BF16 = jnp.bfloat16
F32 = jnp.float32


def halves(value):
    high = value.astype(BF16)
    return high, (value - high.astype(F32)).astype(BF16)


def offsets(count):
    return sorted(range(count), key=lambda k: -min(k, count - k))


def place(me, nx, ny, dx, dy):
    return (lax.rem(me[0] + dx, nx), lax.rem(me[1] + dy, ny))


PAD = 8


def greet(nx, ny, me):
    barrier = pltpu.get_barrier_semaphore()
    for dx in range(nx):
        for dy in range(ny):
            if dx or dy:
                pl.semaphore_signal(barrier, inc=1, device_id=place(me, nx, ny, dx, dy))


def turn_rows(first, count, noise_ref, x_ref, buf):
    height, width, samples = noise_ref.shape
    lines = samples // 2
    low = lax.broadcasted_iota(jnp.int32, (lines, LANES), 1) < width

    def turn(q, _):
        row = first + 2 * q
        both = noise_ref[pl.ds(row, 2)].astype(F32).reshape(2 * width, samples)
        both = both.T
        upper, lower = both[:lines], both[lines:]
        one = jnp.where(low, upper, pltpu.roll(lower, width, 1))
        two = jnp.where(low, pltpu.roll(upper, width, 1), lower)
        buf[pl.ds(row, lines, stride=height + PAD), :] = one
        buf[pl.ds(row + 1, lines, stride=height + PAD), :] = two
        return 0

    lax.fori_loop(0, count // 2, turn, 0, unroll=4)

    def settle(p, _):
        start = pl.multiple_of(p * (height + PAD) + first, 8)
        x_ref[p, first : first + count] = buf[pl.ds(start, count), :].astype(BF16)
        return 0

    lax.fori_loop(0, lines, settle, 0, unroll=8)


def pack_small(tracks, height, rows_ref, dx_ref, kx_ref, dy_ref, ky_ref, obs_ref, w_ref, px_ref, py_ref):
    px_ref[...] = jnp.concatenate([dx_ref[...], kx_ref[...].astype(F32)], axis=1).astype(BF16)
    py_ref[:height] = jnp.concatenate([dy_ref[...], ky_ref[...].astype(F32)], axis=1).astype(BF16)
    at = lax.axis_index("gy")
    per = rows_ref.shape[0]
    lane = lax.broadcasted_iota(jnp.int32, (height, tracks), 1)
    line = lax.broadcasted_iota(jnp.int32, (height, tracks), 0) + at * height
    hot = jnp.zeros((height, tracks), F32)
    for t in range(per):
        hot = hot + jnp.where((lane == at * per + t) & (line == rows_ref[t]), 1.0, 0.0)
    weight = w_ref[...].T
    high = weight.astype(BF16).astype(F32)
    pad = jnp.zeros((height, LANES - 3 * tracks), F32)
    parts = [high, weight - high, hot] + ([pad] if pad.shape[1] else [])
    py_ref[height : 2 * height] = jnp.concatenate(parts, axis=1).astype(BF16)
    obs = obs_ref[...]
    top = obs.astype(BF16).astype(F32)
    obs = jnp.concatenate([top, obs - top], axis=1)
    if per % 16:
        obs = jnp.concatenate([obs, jnp.zeros((-per % 16, LANES), F32)], axis=0)
    py_ref[2 * height :] = obs.astype(BF16)


def unpack_kernel(per, y_ref, gys_ref, w_ref, out_ref, level, buf):
    lines, chunk, _ = y_ref.shape
    height = level.shape[0]
    width = out_ref.shape[1]
    step = pl.program_id(0)

    @pl.when(step == 0)
    def _():
        ny = gys_ref.shape[0]
        seen = [gys_ref[c, 2 * height :].astype(F32)[:per] for c in range(ny)]
        seen = jnp.concatenate(seen, axis=0)
        seen = seen + pltpu.roll(seen, width, 1)
        level[...] = lax.dot_general(
            w_ref[...], seen, (((0,), (0,)), ((), ())), precision=lax.Precision.HIGHEST, preferred_element_type=F32
        )

    add = level[pl.ds(pl.multiple_of(step * chunk, chunk), chunk), :]

    def spread(p, _):
        buf[pl.ds(pl.multiple_of(p * (chunk + PAD), 8), chunk), :] = y_ref[p].astype(F32) + add
        return 0

    lax.fori_loop(0, lines, spread, 0, unroll=16)
    low = lax.broadcasted_iota(jnp.int32, (width, LANES), 1) < lines
    for q in range(chunk // 2):
        one = buf[pl.ds(2 * q, lines, stride=chunk + PAD), :]
        two = buf[pl.ds(2 * q + 1, lines, stride=chunk + PAD), :]
        both = jnp.concatenate([one, two], axis=0).T
        first, second = both[:width], both[width:]
        out_ref[2 * q] = jnp.where(low, first, pltpu.roll(second, lines, 1))
        out_ref[2 * q + 1] = jnp.where(low, pltpu.roll(first, lines, 1), second)


def dot(a, b):
    return jnp.dot(a, b, preferred_element_type=F32)


def build_weights(nx, ny, width, tracks, gxs_ref, gys_ref, wx_ref, wy_ref, wp_ref):
    zero = jnp.zeros((width, width), F32)
    wx_ref[...] = jnp.zeros_like(wx_ref)
    wy_ref[...] = jnp.zeros_like(wy_ref)

    def put_x(out, inn, value):
        row = (inn - (out // 2 * 2 - 1)) * LANES
        lane = (out % 2) * LANES
        for half in range(2):
            sides = [value, zero] if half == 0 else [zero, value]
            wx_ref[out // 2, row + half * width : row + (half + 1) * width, lane : lane + LANES] = (
                jnp.concatenate(sides, axis=1).astype(BF16)
            )

    for b in range(nx):
        both = gxs_ref[b].astype(F32)
        turned = both.T
        put_x(b, b, turned[:width])
        if b:
            put_x(b, b - 1, turned[width:])
            put_x(b - 1, b, both[:, width:])
    blocks = [gys_ref[c, :width].astype(F32) for c in range(ny)]
    for c in range(ny):
        row = [zero] * ny
        row[c] = blocks[c][:, :width]
        if c:
            row[c - 1] = blocks[c][:, width:]
        if c < ny - 1:
            row[c + 1] = blocks[c + 1].T[width:]
        wy_ref[c * width : (c + 1) * width] = jnp.concatenate(row, axis=1).astype(BF16)
    extra = jnp.concatenate([gys_ref[c, width : 2 * width] for c in range(ny)], axis=0)
    hot = extra[:, 2 * tracks : 3 * tracks]
    for part in range(2):
        wp_ref[part] = lax.dot_general(
            extra[:, part * tracks : (part + 1) * tracks], hot, (((1,), (1,)), ((), ())),
            preferred_element_type=F32,
        ).astype(BF16)


def chebyshev(terms, wide, coeff_ref, wx_ref, wy_ref, wp_ref, cur, prev, total, u, cbf, ubf, emit):
    slab = 2 * LANES
    count = wide // slab
    cols = [slice(j * slab, (j + 1) * slab) for j in range(count)]

    def step(k, _):
        twice = jnp.where(k == 1, 1.0, 2.0)
        keep = jnp.where(k == 1, 0.0, 1.0)
        coeff = coeff_ref[k]
        for j in range(count):
            out = NUGGET * cur[:, cols[j]] + dot(cbf[:, j * slab : (j + 2) * slab], wx_ref[j])
            u[:, cols[j]] = out
            ubf[:, cols[j]] = out.astype(BF16)
        for j in range(count):
            out = NUGGET * u[:, cols[j]] + dot(wy_ref[...], ubf[:, cols[j]])
            old = cur[:, cols[j]]
            new = twice * out - keep * prev[:, cols[j]]
            prev[:, cols[j]] = old
            cur[:, cols[j]] = new
            total[:, cols[j]] += coeff * new
            cbf[:, LANES + j * slab : LANES + (j + 1) * slab] = new.astype(BF16)
        return 0

    lax.fori_loop(1, terms, step, 0)
    for j in range(count):
        field = total[:, cols[j]]
        high, low = halves(field)
        fix = dot(wp_ref[0], high) + dot(wp_ref[0], low) + dot(wp_ref[1], high)
        emit(cols[j], field - fix)


def main_kernel(nx, ny, width, tracks, rows_ref, coeff_ref, noise_hbm, dx_ref, kx_ref, dy_ref, ky_ref, obs_ref, w_ref,
                y_ref, gys_ref, noise_ref, buf, x_ref, gx_ref, gy_ref, v_ref, out_ref, gxs_ref, wx_ref, wy_ref, wp_ref, cur, prev, total, u, cbf, ubf,
                load, local, send, recv, early, first, back, home, xsend, xrecv, fsend, frecv, ysend, yrecv):
    me = (lax.axis_index("gx"), lax.axis_index("gy"))
    pairs, tall, wide = v_ref.shape
    height = tall // ny

    def line(at, pair):
        return (at[0] * ny + at[1]) * pairs + pair

    def tile(ref, at, pair):
        return ref.at[pair, pl.ds(pl.multiple_of(at[1] * height, height), height), pl.ds(pl.multiple_of(at[0] * LANES, LANES), LANES)]

    half = height // 2
    quarter = width // ny
    loads = []
    for part in range(2):
        rows = pl.ds(part * half, half)
        loads.append(pltpu.make_async_copy(noise_hbm.at[rows], noise_ref.at[rows], load.at[part]))
        loads[part].start()
    greet(nx, ny, me)
    pack_small(tracks, height, rows_ref, dx_ref, kx_ref, dy_ref, ky_ref, obs_ref, w_ref, gx_ref, gy_ref)
    loads[0].wait()
    turn_rows(0, half, noise_ref, x_ref, buf)
    pl.semaphore_wait(pltpu.get_barrier_semaphore(), nx * ny - 1)
    slot = pl.ds(pl.multiple_of(me[1] * quarter, quarter), quarter)

    def piece(dx, dy, at):
        to = place(me, nx, ny, dx, dy)
        start = pl.multiple_of(at[1] * height, height)
        return pltpu.make_async_remote_copy(
            src_ref=x_ref.at[line(to, 0), pl.ds(0, half)],
            dst_ref=v_ref.at[0, pl.ds(start, half), pl.ds(pl.multiple_of(at[0] * LANES, LANES), LANES)],
            send_sem=early.at[dx * ny + dy], recv_sem=first.at[dx * ny + dy], device_id=to,
        )

    def block(dx, dy, pair, at):
        to = place(me, nx, ny, dx, dy)
        source, target = x_ref.at[line(to, pair)], tile(v_ref, at, pair)
        if pair == 0:
            start = pl.multiple_of(at[1] * height + half, half)
            source = x_ref.at[line(to, 0), pl.ds(half, half)]
            target = v_ref.at[0, pl.ds(start, half), pl.ds(pl.multiple_of(at[0] * LANES, LANES), LANES)]
        return pltpu.make_async_remote_copy(
            src_ref=source, dst_ref=target,
            send_sem=send.at[pair, dx * ny + dy], recv_sem=recv.at[pair, dx * ny + dy], device_id=to,
        )

    def result(dx, dy, pair, at):
        to = place(me, nx, ny, dx, dy)
        return pltpu.make_async_remote_copy(
            src_ref=tile(out_ref, to, pair), dst_ref=y_ref.at[line(at, pair)],
            send_sem=back.at[pair, dx * ny + dy], recv_sem=home.at[pair, dx * ny + dy], device_id=to,
        )

    def part_x(dx, at):
        return pltpu.make_async_remote_copy(
            src_ref=gx_ref.at[slot], dst_ref=gxs_ref.at[at[0], slot], send_sem=xsend.at[dx], recv_sem=xrecv.at[dx],
            device_id=place(me, nx, ny, dx, 0),
        )

    def part_y(dy, at):
        return pltpu.make_async_remote_copy(
            src_ref=gy_ref, dst_ref=gys_ref.at[at[1]], send_sem=ysend.at[dy], recv_sem=yrecv.at[dy],
            device_id=place(me, nx, ny, 0, dy),
        )

    def spread_x(dy, at):
        spot = pl.ds(pl.multiple_of(at[1] * quarter, quarter), quarter)
        return pltpu.make_async_remote_copy(
            src_ref=gxs_ref.at[:, spot], dst_ref=gxs_ref.at[:, spot], send_sem=fsend.at[dy], recv_sem=frecv.at[dy],
            device_id=place(me, nx, ny, 0, dy),
        )

    order = [(dx, dy) for dx in offsets(nx) for dy in offsets(ny) if dx or dy]
    for dx in offsets(nx):
        if dx:
            part_x(dx, me).start()
    for dx, dy in order:
        piece(dx, dy, me).start()
    for dy in offsets(ny):
        if dy:
            part_y(dy, me).start()
    own = [
        pltpu.make_async_copy(gx_ref.at[slot], gxs_ref.at[me[0], slot], local.at[0]),
        pltpu.make_async_copy(gy_ref, gys_ref.at[me[1]], local.at[1]),
    ]
    for copy in own:
        copy.start()
    loads[1].wait()
    turn_rows(half, half, noise_ref, x_ref, buf)
    for pair in range(pairs):
        for dx, dy in order:
            block(dx, dy, pair, me).start()
        own.append(pltpu.make_async_copy(x_ref.at[line(me, pair)], tile(v_ref, me, pair), local.at[2 + pair]))
        own[-1].start()
    own[0].wait()
    own[1].wait()
    for dx in offsets(nx):
        if dx:
            part_x(dx, place(me, nx, ny, nx - dx, 0)).wait()
    for dy in offsets(ny):
        if dy:
            spread_x(dy, me).start()
    for dy in offsets(ny):
        if dy:
            part_y(dy, place(me, nx, ny, 0, ny - dy)).wait()
    for dy in offsets(ny):
        if dy:
            spread_x(dy, me).wait_send()
            spread_x(dy, place(me, nx, ny, 0, ny - dy)).wait_recv()
    build_weights(nx, ny, width, tracks, gxs_ref, gys_ref, wx_ref, wy_ref, wp_ref)
    cbf[:, :LANES] = jnp.zeros((tall, LANES), BF16)
    cbf[:, LANES + wide :] = jnp.zeros((tall, LANES), BF16)
    mine = []
    for pair in range(pairs):
        own[2 + pair].wait()
        if pair == 0:
            for dx, dy in order:
                piece(dx, dy, place(me, nx, ny, nx - dx, ny - dy)).wait()
        for dx, dy in order:
            block(dx, dy, pair, place(me, nx, ny, nx - dx, ny - dy)).wait()
        value = v_ref[pair]
        cbf[:, LANES : LANES + wide] = value
        start = value.astype(F32)
        cur[...] = start
        prev[...] = start
        total[...] = coeff_ref[0] * start

        def emit(col, value, pair=pair):
            out_ref[pair, :, col] = value.astype(BF16)

        chebyshev(coeff_ref.shape[0], wide, coeff_ref, wx_ref, wy_ref, wp_ref, cur, prev, total, u, cbf, ubf, emit)
        for dx, dy in order:
            result(dx, dy, pair, me).start()
        mine.append(pltpu.make_async_copy(tile(out_ref, me, pair), y_ref.at[line(me, pair)], local.at[2 + pair]))
        mine[-1].start()
    for pair in range(pairs):
        for dx, dy in order:
            result(dx, dy, pair, place(me, nx, ny, nx - dx, ny - dy)).wait()
        mine[pair].wait()


def swap_body(nx, ny, noise, cheb_coeff, diag_x, couple_x, diag_y, couple_y, track_rows, track_obs, weights):
    height, width, samples = noise.shape
    tracks = weights.shape[1]
    per = track_rows.shape[0]
    lines = samples // 2
    devices = nx * ny
    pairs = lines // devices
    tall, wide = ny * height, nx * LANES
    rows = 2 * height + per + -per % 16
    vmem = pl.BlockSpec(memory_space=pltpu.VMEM)
    smem = pl.BlockSpec(memory_space=pltpu.SMEM)
    dma = pltpu.SemaphoreType.DMA
    mixed = pltpu.VMEM((lines * (height + PAD), LANES), F32)
    field = pltpu.VMEM((tall, wide), F32)
    half = pltpu.VMEM((pairs, tall, wide), BF16)
    y, gys = pl.pallas_call(
        lambda *refs: main_kernel(nx, ny, width, tracks, *refs),
        out_shape=(
            jax.ShapeDtypeStruct((lines, height, LANES), BF16),
            jax.ShapeDtypeStruct((ny, rows, LANES), BF16),
        ),
        in_specs=[smem, smem, pl.BlockSpec(memory_space=pl.ANY)] + [vmem] * 6,
        out_specs=(pl.BlockSpec(memory_space=pl.ANY), vmem),
        scratch_shapes=[
            pltpu.VMEM((height, width, samples), BF16),
            mixed,
            pltpu.VMEM((lines, height, LANES), BF16),
            pltpu.VMEM((width, LANES), BF16),
            pltpu.VMEM((rows, LANES), BF16),
            half, half,
            pltpu.VMEM((nx, width, LANES), BF16),
            pltpu.VMEM((nx // 2, 4 * LANES, 2 * LANES), BF16),
            pltpu.VMEM((tall, tall), BF16),
            pltpu.VMEM((2, tall, tall), BF16),
            field, field, field, field,
            pltpu.VMEM((tall, wide + 2 * LANES), BF16),
            pltpu.VMEM((tall, wide), BF16),
            dma((2,)), dma((pairs + 2,)),
            dma((pairs, devices)), dma((pairs, devices)), dma((devices,)), dma((devices,)),
            dma((pairs, devices)), dma((pairs, devices)),
            dma((nx,)), dma((nx,)), dma((ny,)), dma((ny,)), dma((ny,)), dma((ny,)),
        ],
        compiler_params=pltpu.CompilerParams(collective_id=0, has_side_effects=True),
        name="swap",
    )(track_rows, cheb_coeff, noise, diag_x, couple_x, diag_y, couple_y, track_obs, weights.T)
    chunk = height // 2
    return pl.pallas_call(
        lambda *refs: unpack_kernel(per, *refs),
        grid=(height // chunk,),
        out_shape=jax.ShapeDtypeStruct((height, width, samples), F32),
        in_specs=[pl.BlockSpec((lines, chunk, LANES), lambda i: (0, i, 0)), vmem, vmem],
        out_specs=pl.BlockSpec((chunk, width, samples), lambda i: (i, 0, 0)),
        scratch_shapes=[pltpu.VMEM((height, LANES), F32), pltpu.VMEM((lines * (chunk + PAD), LANES), F32)],
        name="unpack",
    )(y, gys, weights.T)


def body(noise, *rest):
    nx, ny = lax.axis_size("gx"), lax.axis_size("gy")
    height, width, samples = noise.shape
    tracks, per = rest[-1].shape[1], rest[-3].shape[0]
    fits = 2 * width == LANES and height == width and nx % 2 == 0 and samples % (2 * nx * ny) == 0 and samples == LANES
    fits = fits and width % (16 * ny) == 0 and 3 * tracks <= LANES and per * ny == tracks
    if fits:
        return swap_body(nx, ny, noise, *rest)
    return halo_body(noise, *rest)


def solution(mesh):
    return jax.shard_map(
        body,
        mesh=mesh,
        in_specs=(
            P("gy", "gx", None),
            P(),
            P("gx", None),
            P("gx", None),
            P("gy", None),
            P("gy", None),
            P("gy"),
            P("gy", "gx"),
            P("gy", None),
        ),
        out_specs=P("gy", "gx", None),
        check_vma=False,
    )
```

```python
import jax
import jax.numpy as jnp
from jax import lax
from jax.experimental import pallas as pl
from jax.experimental.pallas import tpu as pltpu
from jax.sharding import PartitionSpec as P

NUGGET = 0.3


def padded_2(value, sides, width):
    for axis, dim in sides:
        size, length = (lax.axis_size(axis), value.shape[dim])
        up = [(i, (i + 1) % size) for i in range(size - 1)]
        down = [(j, i) for i, j in up]
        last = lax.slice_in_dim(value, length - width, length, axis=dim)
        leading = lax.slice_in_dim(value, 0, width, axis=dim)
        before = lax.ppermute(last, axis, up)
        after = lax.ppermute(leading, axis, down)
        value = jnp.concatenate([before, value, after], axis=dim)
    return value


def shifted(value, axis, steps):
    count = lax.axis_size(axis)
    leading, last = (max(0, -steps), min(count, count - steps))
    return lax.ppermute(value, axis, [(source, source + steps) for source in range(leading, last)])


def along_rows(matrix, field):
    return jnp.einsum("ij,yjs->yis", matrix, field, preferred_element_type=jnp.float32)


def along_rows_back(matrix, field):
    return jnp.einsum("ji,yjs->yis", matrix, field, preferred_element_type=jnp.float32)


def along_cols(matrix, field):
    flat = field.reshape(field.shape[0], -1)
    return jnp.dot(matrix, flat, preferred_element_type=jnp.float32).reshape(field.shape)


def along_cols_back(matrix, field):
    flat = field.reshape(field.shape[0], -1)
    return jnp.dot(matrix.T, flat, preferred_element_type=jnp.float32).reshape(field.shape)


def apply_rows(field, diag_x, couple_x, next_x):
    width = field.shape[1]
    own = NUGGET * field + jnp.einsum(
        "ij,yjs->yis",
        diag_x,
        field,
        precision=lax.Precision.HIGHEST,
        preferred_element_type=jnp.float32,
    )
    rounded = field.astype(jnp.bfloat16)
    padded = padded_2(rounded, (("gx", 1),), width)
    from_prev = along_rows(couple_x, padded[:, :width]).astype(jnp.bfloat16)
    from_next = along_rows_back(next_x, padded[:, 2 * width :]).astype(jnp.bfloat16)
    from_prev = lax.optimization_barrier(from_prev)
    from_next = lax.optimization_barrier(from_next)
    return own + from_prev.astype(jnp.float32) + from_next.astype(jnp.float32)


def apply_cols(field, diag_y, couple_y, next_y):
    height = field.shape[0]
    own = NUGGET * field + jnp.dot(
        diag_y,
        field.reshape(height, -1),
        precision=lax.Precision.HIGHEST,
        preferred_element_type=jnp.float32,
    ).reshape(field.shape)
    rounded = field.astype(jnp.bfloat16)
    padded = padded_2(rounded, (("gy", 0),), height)
    from_prev = along_cols(couple_y, padded[:height]).astype(jnp.bfloat16)
    from_next = along_cols_back(next_y, padded[2 * height :]).astype(jnp.bfloat16)
    from_prev = lax.optimization_barrier(from_prev)
    from_next = lax.optimization_barrier(from_next)
    return own + from_prev.astype(jnp.float32) + from_next.astype(jnp.float32)


def halo_body(noise, cheb_coeff, diag_x, couple_x, diag_y, couple_y, track_rows, track_obs, weights):
    next_x = shifted(couple_x, "gx", -1)
    next_y = shifted(couple_y, "gy", -1)

    def operator(field):
        return apply_cols(apply_rows(field, diag_x, couple_x, next_x), diag_y, couple_y, next_y)

    start = noise.astype(jnp.float32)
    terms = cheb_coeff.shape[0]
    previous = start
    current = operator(start)
    total = cheb_coeff[0] * start
    total = total + cheb_coeff[1] * current
    for term in range(2, terms):
        following = 2.0 * operator(current) - previous
        previous = current
        current = following
        total = total + cheb_coeff[term] * current
    height = total.shape[0]
    first_row = lax.axis_index("gy") * height
    local_rows = track_rows - first_row
    picked = jnp.take(total, local_rows, axis=0)
    misfit = picked - track_obs[:, :, None]
    piece = lax.all_gather(misfit.astype(jnp.bfloat16), "gy", axis=0, tiled=True).astype(
        jnp.float32
    )
    flat = piece.reshape(piece.shape[0], -1)
    correction = jnp.dot(
        weights, flat, precision=lax.Precision.HIGHEST, preferred_element_type=jnp.float32
    )
    return total - correction.reshape(total.shape)

LANES = 128
BF16 = jnp.bfloat16
F32 = jnp.float32


def halves(value):
    high = value.astype(BF16)
    return high, (value - high.astype(F32)).astype(BF16)


def offsets(count):
    return sorted(range(count), key=lambda k: -min(k, count - k))


def place(me, nx, ny, dx, dy):
    return (lax.rem(me[0] + dx, nx), lax.rem(me[1] + dy, ny))


PAD = 8


def greet(nx, ny, me):
    barrier = pltpu.get_barrier_semaphore()
    for dx in range(nx):
        for dy in range(ny):
            if dx or dy:
                pl.semaphore_signal(barrier, inc=1, device_id=place(me, nx, ny, dx, dy))


def turn_rows(first, count, noise_ref, x_ref, buf):
    height, width, samples = noise_ref.shape
    lines = samples // 2
    low = lax.broadcasted_iota(jnp.int32, (lines, LANES), 1) < width

    def turn(q, _):
        row = first + 2 * q
        both = noise_ref[pl.ds(row, 2)].astype(F32).reshape(2 * width, samples)
        both = both.T
        upper, lower = both[:lines], both[lines:]
        one = jnp.where(low, upper, pltpu.roll(lower, width, 1))
        two = jnp.where(low, pltpu.roll(upper, width, 1), lower)
        buf[pl.ds(row, lines, stride=height + PAD), :] = one
        buf[pl.ds(row + 1, lines, stride=height + PAD), :] = two
        return 0

    lax.fori_loop(0, count // 2, turn, 0, unroll=4)

    def settle(p, _):
        start = pl.multiple_of(p * (height + PAD) + first, 8)
        x_ref[p, first : first + count] = buf[pl.ds(start, count), :].astype(BF16)
        return 0

    lax.fori_loop(0, lines, settle, 0, unroll=8)


def pack_small(tracks, height, rows_ref, dx_ref, kx_ref, dy_ref, ky_ref, obs_ref, w_ref, px_ref, py_ref):
    px_ref[...] = jnp.concatenate([dx_ref[...], kx_ref[...].astype(F32)], axis=1).astype(BF16)
    py_ref[:height] = jnp.concatenate([dy_ref[...], ky_ref[...].astype(F32)], axis=1).astype(BF16)
    at = lax.axis_index("gy")
    per = rows_ref.shape[0]
    lane = lax.broadcasted_iota(jnp.int32, (height, tracks), 1)
    line = lax.broadcasted_iota(jnp.int32, (height, tracks), 0) + at * height
    hot = jnp.zeros((height, tracks), F32)
    for t in range(per):
        hot = hot + jnp.where((lane == at * per + t) & (line == rows_ref[t]), 1.0, 0.0)
    weight = w_ref[...].T
    high = weight.astype(BF16).astype(F32)
    pad = jnp.zeros((height, LANES - 3 * tracks), F32)
    parts = [high, weight - high, hot] + ([pad] if pad.shape[1] else [])
    py_ref[height : 2 * height] = jnp.concatenate(parts, axis=1).astype(BF16)
    obs = obs_ref[...]
    top = obs.astype(BF16).astype(F32)
    obs = jnp.concatenate([top, obs - top], axis=1)
    if per % 16:
        obs = jnp.concatenate([obs, jnp.zeros((-per % 16, LANES), F32)], axis=0)
    py_ref[2 * height :] = obs.astype(BF16)


def unpack_kernel(per, y_ref, gys_ref, w_ref, out_ref, level, buf):
    lines, chunk, _ = y_ref.shape
    height = level.shape[0]
    width = out_ref.shape[1]
    step = pl.program_id(0)

    @pl.when(step == 0)
    def _():
        ny = gys_ref.shape[0]
        seen = [gys_ref[c, 2 * height :].astype(F32)[:per] for c in range(ny)]
        seen = jnp.concatenate(seen, axis=0)
        seen = seen + pltpu.roll(seen, width, 1)
        level[...] = lax.dot_general(
            w_ref[...], seen, (((0,), (0,)), ((), ())), precision=lax.Precision.HIGHEST, preferred_element_type=F32
        )

    add = level[pl.ds(pl.multiple_of(step * chunk, chunk), chunk), :]

    def spread(p, _):
        buf[pl.ds(pl.multiple_of(p * (chunk + PAD), 8), chunk), :] = y_ref[p].astype(F32) + add
        return 0

    lax.fori_loop(0, lines, spread, 0, unroll=16)
    low = lax.broadcasted_iota(jnp.int32, (width, LANES), 1) < lines
    for q in range(chunk // 2):
        one = buf[pl.ds(2 * q, lines, stride=chunk + PAD), :]
        two = buf[pl.ds(2 * q + 1, lines, stride=chunk + PAD), :]
        both = jnp.concatenate([one, two], axis=0).T
        first, second = both[:width], both[width:]
        out_ref[2 * q] = jnp.where(low, first, pltpu.roll(second, lines, 1))
        out_ref[2 * q + 1] = jnp.where(low, pltpu.roll(first, lines, 1), second)


def dot(a, b):
    return jnp.dot(a, b, preferred_element_type=F32)


def build_weights(nx, ny, width, tracks, gxs_ref, gys_ref, wx_ref, wy_ref, wp_ref):
    zero = jnp.zeros((width, width), F32)
    wx_ref[...] = jnp.zeros_like(wx_ref)
    wy_ref[...] = jnp.zeros_like(wy_ref)

    def put_x(out, inn, value):
        row = (inn - (out // 2 * 2 - 1)) * LANES
        lane = (out % 2) * LANES
        for half in range(2):
            sides = [value, zero] if half == 0 else [zero, value]
            wx_ref[out // 2, row + half * width : row + (half + 1) * width, lane : lane + LANES] = (
                jnp.concatenate(sides, axis=1).astype(BF16)
            )

    for b in range(nx):
        both = gxs_ref[b].astype(F32)
        turned = both.T
        put_x(b, b, turned[:width])
        if b:
            put_x(b, b - 1, turned[width:])
            put_x(b - 1, b, both[:, width:])
    blocks = [gys_ref[c, :width].astype(F32) for c in range(ny)]
    for c in range(ny):
        row = [zero] * ny
        row[c] = blocks[c][:, :width]
        if c:
            row[c - 1] = blocks[c][:, width:]
        if c < ny - 1:
            row[c + 1] = blocks[c + 1].T[width:]
        wy_ref[c * width : (c + 1) * width] = jnp.concatenate(row, axis=1).astype(BF16)
    extra = jnp.concatenate([gys_ref[c, width : 2 * width] for c in range(ny)], axis=0)
    hot = extra[:, 2 * tracks : 3 * tracks]
    for part in range(2):
        wp_ref[part] = lax.dot_general(
            extra[:, part * tracks : (part + 1) * tracks], hot, (((1,), (1,)), ((), ())),
            preferred_element_type=F32,
        ).astype(BF16)


def chebyshev(terms, wide, coeff_ref, wx_ref, wy_ref, wp_ref, cur, prev, total, u, cbf, ubf, emit):
    slab = 2 * LANES
    count = wide // slab
    cols = [slice(j * slab, (j + 1) * slab) for j in range(count)]

    def step(k, _):
        twice = jnp.where(k == 1, 1.0, 2.0)
        keep = jnp.where(k == 1, 0.0, 1.0)
        coeff = coeff_ref[k]
        for j in range(count):
            out = NUGGET * cur[:, cols[j]] + dot(cbf[:, j * slab : (j + 2) * slab], wx_ref[j])
            u[:, cols[j]] = out
            ubf[:, cols[j]] = out.astype(BF16)
        for j in range(count):
            out = NUGGET * u[:, cols[j]] + dot(wy_ref[...], ubf[:, cols[j]])
            old = cur[:, cols[j]]
            new = twice * out - keep * prev[:, cols[j]]
            prev[:, cols[j]] = old
            cur[:, cols[j]] = new
            total[:, cols[j]] += coeff * new
            cbf[:, LANES + j * slab : LANES + (j + 1) * slab] = new.astype(BF16)
        return 0

    lax.fori_loop(1, terms, step, 0)
    for j in range(count):
        field = total[:, cols[j]]
        high, low = halves(field)
        fix = dot(wp_ref[0], high) + dot(wp_ref[0], low) + dot(wp_ref[1], high)
        emit(cols[j], field - fix)


def main_kernel(nx, ny, width, tracks, rows_ref, coeff_ref, noise_hbm, dx_ref, kx_ref, dy_ref, ky_ref, obs_ref, w_ref,
                y_ref, gys_ref, noise_ref, buf, x_ref, gx_ref, gy_ref, v_ref, out_ref, gxs_ref, wx_ref, wy_ref, wp_ref, cur, prev, total, u, cbf, ubf,
                load, local, send, recv, early, first, back, home, xsend, xrecv, fsend, frecv, ysend, yrecv):
    me = (lax.axis_index("gx"), lax.axis_index("gy"))
    pairs, tall, wide = v_ref.shape
    height = tall // ny

    def line(at, pair):
        return (at[0] * ny + at[1]) * pairs + pair

    def tile(ref, at, pair):
        return ref.at[pair, pl.ds(pl.multiple_of(at[1] * height, height), height), pl.ds(pl.multiple_of(at[0] * LANES, LANES), LANES)]

    half = height // 2
    quarter = width // ny
    loads = []
    for part in range(2):
        rows = pl.ds(part * half, half)
        loads.append(pltpu.make_async_copy(noise_hbm.at[rows], noise_ref.at[rows], load.at[part]))
        loads[part].start()
    greet(nx, ny, me)
    pack_small(tracks, height, rows_ref, dx_ref, kx_ref, dy_ref, ky_ref, obs_ref, w_ref, gx_ref, gy_ref)
    loads[0].wait()
    turn_rows(0, half, noise_ref, x_ref, buf)
    pl.semaphore_wait(pltpu.get_barrier_semaphore(), nx * ny - 1)
    slot = pl.ds(pl.multiple_of(me[1] * quarter, quarter), quarter)

    def piece(dx, dy, at):
        to = place(me, nx, ny, dx, dy)
        start = pl.multiple_of(at[1] * height, height)
        return pltpu.make_async_remote_copy(
            src_ref=x_ref.at[line(to, 0), pl.ds(0, half)],
            dst_ref=v_ref.at[0, pl.ds(start, half), pl.ds(pl.multiple_of(at[0] * LANES, LANES), LANES)],
            send_sem=early.at[dx * ny + dy], recv_sem=first.at[dx * ny + dy], device_id=to,
        )

    def block(dx, dy, pair, at):
        to = place(me, nx, ny, dx, dy)
        source, target = x_ref.at[line(to, pair)], tile(v_ref, at, pair)
        if pair == 0:
            start = pl.multiple_of(at[1] * height + half, half)
            source = x_ref.at[line(to, 0), pl.ds(half, half)]
            target = v_ref.at[0, pl.ds(start, half), pl.ds(pl.multiple_of(at[0] * LANES, LANES), LANES)]
        return pltpu.make_async_remote_copy(
            src_ref=source, dst_ref=target,
            send_sem=send.at[pair, dx * ny + dy], recv_sem=recv.at[pair, dx * ny + dy], device_id=to,
        )

    def result(dx, dy, pair, at):
        to = place(me, nx, ny, dx, dy)
        return pltpu.make_async_remote_copy(
            src_ref=tile(out_ref, to, pair), dst_ref=y_ref.at[line(at, pair)],
            send_sem=back.at[pair, dx * ny + dy], recv_sem=home.at[pair, dx * ny + dy], device_id=to,
        )

    def part_x(dx, at):
        return pltpu.make_async_remote_copy(
            src_ref=gx_ref.at[slot], dst_ref=gxs_ref.at[at[0], slot], send_sem=xsend.at[dx], recv_sem=xrecv.at[dx],
            device_id=place(me, nx, ny, dx, 0),
        )

    def part_y(dy, at):
        return pltpu.make_async_remote_copy(
            src_ref=gy_ref, dst_ref=gys_ref.at[at[1]], send_sem=ysend.at[dy], recv_sem=yrecv.at[dy],
            device_id=place(me, nx, ny, 0, dy),
        )

    def spread_x(dy, at):
        spot = pl.ds(pl.multiple_of(at[1] * quarter, quarter), quarter)
        return pltpu.make_async_remote_copy(
            src_ref=gxs_ref.at[:, spot], dst_ref=gxs_ref.at[:, spot], send_sem=fsend.at[dy], recv_sem=frecv.at[dy],
            device_id=place(me, nx, ny, 0, dy),
        )

    order = [(dx, dy) for dx in offsets(nx) for dy in offsets(ny) if dx or dy]
    for dx in offsets(nx):
        if dx:
            part_x(dx, me).start()
    for dx, dy in order:
        piece(dx, dy, me).start()
    for dy in offsets(ny):
        if dy:
            part_y(dy, me).start()
    own = [
        pltpu.make_async_copy(gx_ref.at[slot], gxs_ref.at[me[0], slot], local.at[0]),
        pltpu.make_async_copy(gy_ref, gys_ref.at[me[1]], local.at[1]),
    ]
    for copy in own:
        copy.start()
    loads[1].wait()
    turn_rows(half, half, noise_ref, x_ref, buf)
    for pair in range(pairs):
        for dx, dy in order:
            block(dx, dy, pair, me).start()
        own.append(pltpu.make_async_copy(x_ref.at[line(me, pair)], tile(v_ref, me, pair), local.at[2 + pair]))
        own[-1].start()
    own[0].wait()
    own[1].wait()
    for dx in offsets(nx):
        if dx:
            part_x(dx, place(me, nx, ny, nx - dx, 0)).wait()
    for dy in offsets(ny):
        if dy:
            spread_x(dy, me).start()
    for dy in offsets(ny):
        if dy:
            part_y(dy, place(me, nx, ny, 0, ny - dy)).wait()
    for dy in offsets(ny):
        if dy:
            spread_x(dy, me).wait_send()
            spread_x(dy, place(me, nx, ny, 0, ny - dy)).wait_recv()
    build_weights(nx, ny, width, tracks, gxs_ref, gys_ref, wx_ref, wy_ref, wp_ref)
    cbf[:, :LANES] = jnp.zeros((tall, LANES), BF16)
    cbf[:, LANES + wide :] = jnp.zeros((tall, LANES), BF16)
    mine = []
    for pair in range(pairs):
        own[2 + pair].wait()
        if pair == 0:
            for dx, dy in order:
                piece(dx, dy, place(me, nx, ny, nx - dx, ny - dy)).wait()
        for dx, dy in order:
            block(dx, dy, pair, place(me, nx, ny, nx - dx, ny - dy)).wait()
        value = v_ref[pair]
        cbf[:, LANES : LANES + wide] = value
        start = value.astype(F32)
        cur[...] = start
        prev[...] = start
        total[...] = coeff_ref[0] * start

        def emit(col, value, pair=pair):
            out_ref[pair, :, col] = value.astype(BF16)

        chebyshev(coeff_ref.shape[0], wide, coeff_ref, wx_ref, wy_ref, wp_ref, cur, prev, total, u, cbf, ubf, emit)
        for dx, dy in order:
            result(dx, dy, pair, me).start()
        mine.append(pltpu.make_async_copy(tile(out_ref, me, pair), y_ref.at[line(me, pair)], local.at[2 + pair]))
        mine[-1].start()
    for pair in range(pairs):
        for dx, dy in order:
            result(dx, dy, pair, place(me, nx, ny, nx - dx, ny - dy)).wait()
        mine[pair].wait()


def swap_body(nx, ny, noise, cheb_coeff, diag_x, couple_x, diag_y, couple_y, track_rows, track_obs, weights):
    height, width, samples = noise.shape
    tracks = weights.shape[1]
    per = track_rows.shape[0]
    lines = samples // 2
    devices = nx * ny
    pairs = lines // devices
    tall, wide = ny * height, nx * LANES
    rows = 2 * height + per + -per % 16
    vmem = pl.BlockSpec(memory_space=pltpu.VMEM)
    smem = pl.BlockSpec(memory_space=pltpu.SMEM)
    dma = pltpu.SemaphoreType.DMA
    mixed = pltpu.VMEM(((lines + 1) * (height + PAD), LANES), F32)
    field = pltpu.VMEM((tall, wide), F32)
    half = pltpu.VMEM((pairs, tall, wide), BF16)
    y, gys = pl.pallas_call(
        lambda *refs: main_kernel(nx, ny, width, tracks, *refs),
        out_shape=(
            jax.ShapeDtypeStruct((lines, height, LANES), BF16),
            jax.ShapeDtypeStruct((ny, rows, LANES), BF16),
        ),
        in_specs=[smem, smem, pl.BlockSpec(memory_space=pl.ANY)] + [vmem] * 6,
        out_specs=(pl.BlockSpec(memory_space=pl.ANY), vmem),
        scratch_shapes=[
            pltpu.VMEM((height, width, samples), BF16),
            mixed,
            pltpu.VMEM((lines, height, LANES), BF16),
            pltpu.VMEM((width, LANES), BF16),
            pltpu.VMEM((rows, LANES), BF16),
            half, half,
            pltpu.VMEM((nx, width, LANES), BF16),
            pltpu.VMEM((nx // 2, 4 * LANES, 2 * LANES), BF16),
            pltpu.VMEM((tall, tall), BF16),
            pltpu.VMEM((2, tall, tall), BF16),
            field, field, field, field,
            pltpu.VMEM((tall, wide + 2 * LANES), BF16),
            pltpu.VMEM((tall, wide), BF16),
            dma((2,)), dma((pairs + 2,)),
            dma((pairs, devices)), dma((pairs, devices)), dma((devices,)), dma((devices,)),
            dma((pairs, devices)), dma((pairs, devices)),
            dma((nx,)), dma((nx,)), dma((ny,)), dma((ny,)), dma((ny,)), dma((ny,)),
        ],
        compiler_params=pltpu.CompilerParams(collective_id=0, has_side_effects=True),
        name="swap",
    )(track_rows, cheb_coeff, noise, diag_x, couple_x, diag_y, couple_y, track_obs, weights.T)
    chunk = height // 2
    return pl.pallas_call(
        lambda *refs: unpack_kernel(per, *refs),
        grid=(height // chunk,),
        out_shape=jax.ShapeDtypeStruct((height, width, samples), F32),
        in_specs=[pl.BlockSpec((lines, chunk, LANES), lambda i: (0, i, 0)), vmem, vmem],
        out_specs=pl.BlockSpec((chunk, width, samples), lambda i: (i, 0, 0)),
        scratch_shapes=[pltpu.VMEM((height, LANES), F32), pltpu.VMEM(((lines + 1) * (chunk + PAD), LANES), F32)],
        name="unpack",
    )(y, gys, weights.T)


def body(noise, *rest):
    nx, ny = lax.axis_size("gx"), lax.axis_size("gy")
    height, width, samples = noise.shape
    tracks, per = rest[-1].shape[1], rest[-3].shape[0]
    fits = 2 * width == LANES and height == width and nx % 2 == 0 and samples % (2 * nx * ny) == 0 and samples == LANES
    fits = fits and width % (16 * ny) == 0 and 3 * tracks <= LANES and per * ny == tracks
    if fits:
        return swap_body(nx, ny, noise, *rest)
    return halo_body(noise, *rest)


def solution(mesh):
    return jax.shard_map(
        body,
        mesh=mesh,
        in_specs=(
            P("gy", "gx", None),
            P(),
            P("gx", None),
            P("gx", None),
            P("gy", None),
            P("gy", None),
            P("gy"),
            P("gy", "gx"),
            P("gy", None),
        ),
        out_specs=P("gy", "gx", None),
        check_vma=False,
    )
```
